256 devices in a mesh: tok: 8 (over z), out: 16 (over y_lo, x, core), grp: 2 (over y_hi).
Axes of the slice: x: 4, y: 4 (y_hi: 2, y_lo: 2; y = y_hi * 2 + y_lo), z: 8, core: 2. Of those that a mesh axis runs over, the one named last changes fastest.
Arguments:
- activations: bfloat16 [2048, 2, 2048], P(('tok', 'grp'), None, 'out'), may hold values from -16 to 16
- out_grads: bfloat16 [2048, 2, 2048], P(('tok', 'grp'), None, 'out'), may hold values from -16 to 16
- weight: bfloat16 [2, 2048, 4096], P(None, 'out'), may hold values from -0.09375 to 0.09375
Outputs:
- update: bfloat16 [4096, 2, 2048], P(('tok', 'grp'), None, 'out')
- input_grad: bfloat16 [2048, 2, 2048], P(('tok', 'grp'), None, 'out')
The draws below stay inside these ranges and needn't reach their ends.
All inputs are finite; a program needn't handle non-finite values.
Results may differ from the reference program's by a relative error of at most 0.0092.
Values may be sent and summed in bfloat16 or wider, within the bound.
No kernel may reach another device: no remote copies, remote signals or barrier semaphores. Data moves between devices by JAX's collectives and lax.ppermute only.
A program may use at most 64 MiB of HBM per device.

```python
import math
import jax
import jax.numpy as jnp
from jax import lax

BLOCK = 2048
NBLOCKS = 2
POWER = 3
D = 4096
TOKENS = 2048


def shaped_sides(key):
    noise_key, level_key, reach_key, sign_key, turn_key, weight_key, factor_key = jax.random.split(key, 7)
    array_shape = (TOKENS, NBLOCKS, BLOCK)
    bulk_noise = jnp.clip(jax.random.normal(noise_key, array_shape, jnp.float32), -4.0, 4.0)
    strength = jax.random.uniform(factor_key, (NBLOCKS,), jnp.float32, 1.8, 3.0)
    levels = jnp.exp(jax.random.uniform(level_key, (NBLOCKS, BLOCK), jnp.float32, -1.2, 1.2))
    block_reach = jax.random.uniform(reach_key, (NBLOCKS,), jnp.float32, 0.35, 0.7)
    parity = jnp.where(jnp.arange(NBLOCKS) % 2 == 0, 1.0, -1.0)
    block_sign = jnp.where(jax.random.bernoulli(sign_key, 0.5), 1.0, -1.0)
    magnitude = jnp.exp(block_reach * parity * block_sign)
    squares = levels * levels
    orthonormal = []
    for column_vec in (jnp.ones_like(squares), squares, squares * squares):
        for member in orthonormal:
            column_vec = column_vec - jnp.sum(column_vec * member, axis=1, keepdims=True) * member
        orthonormal.append(column_vec / jnp.sqrt(jnp.sum(column_vec * column_vec, axis=1, keepdims=True)))
    direction = jax.random.normal(turn_key, (NBLOCKS, BLOCK), jnp.float32)
    for member in orthonormal:
        direction = direction - jnp.sum(direction * member, axis=1, keepdims=True) * member
    direction = direction / jnp.sqrt(jnp.sum(direction * direction, axis=1, keepdims=True))
    amplitude = jnp.sqrt(strength * 3.0 * jnp.max(squares, axis=1))
    weights = jax.random.normal(weight_key, (TOKENS, NBLOCKS), jnp.float32)
    shaped = magnitude[None, :, None] * (levels[None] * bulk_noise + amplitude[None, :, None] * weights[:, :, None] * direction[None])
    return jnp.clip(shaped, -16.0, 16.0)


def draw_activations(key, part):
    return shaped_sides(jax.random.fold_in(key, 11)).astype(jnp.bfloat16)


def draw_out_grads(key, part):
    return shaped_sides(jax.random.fold_in(key, 23)).astype(jnp.bfloat16)


def shard_levels(rng, extent, shards, low, largest):
    def one(axis_at, blocks):
        steps = jax.random.uniform(jax.random.fold_in(jax.random.fold_in(rng, 6), axis_at), (blocks,), jnp.float32, low / len(shards), largest / len(shards))
        return jnp.repeat(jnp.exp(steps), extent[axis_at] // blocks).reshape((-1,) + (1,) * (len(extent) - axis_at - 1))

    factor_of = one(*shards[0])
    for cut in shards[1:]:
        factor_of = factor_of * one(*cut)
    return factor_of


def gaussian(key, shape, width, limit, cuts=(), kind=jnp.bfloat16):
    result = width * jax.random.normal(key, shape, jnp.float32)
    if cuts:
        result = result * shard_levels(key, shape, cuts, -0.22, 0.18)
    return jnp.clip(result, -limit, limit).astype(kind)


def setup_inputs(seed: int = 0) -> dict:
    seeds = jax.random.split(jax.random.key(seed), 4)
    activations = draw_activations(jax.random.fold_in(seeds[3], 71), 0)
    out_grads = draw_out_grads(jax.random.fold_in(seeds[3], 71), 0)
    weight = gaussian(seeds[2], (NBLOCKS, BLOCK, D), D ** -0.5, 0.09375, ((1, 16),))
    return dict(activations=activations, out_grads=out_grads, weight=weight)


DAMPING = 0.1
HIGH = lax.Precision.HIGHEST

def lowered(value):
    return lax.optimization_barrier(value.astype(jnp.bfloat16))

def batched(left, right):
    return jnp.einsum('kij,kjl->kil', left.astype(jnp.float32), right.astype(jnp.float32), precision=HIGH)

def reference(activations, out_grads, weight):
    sides = jnp.concatenate([activations, out_grads], axis=1)
    wide = sides.astype(jnp.float32)
    tokens = sides.shape[0]
    count = sides.shape[1]
    block = sides.shape[2]
    half = count // 2
    identity = jnp.eye(block, dtype=jnp.float32)[None]
    factor = jnp.einsum('tki,tkj->kij', wide, wide, precision=HIGH) / tokens + DAMPING * identity
    vector = jnp.ones((count, block), jnp.float32)
    image = vector
    for step in range(POWER):
        image = jnp.einsum('kij,kj->ki', factor, vector, precision=HIGH)
        if step + 1 < POWER:
            vector = image / jnp.sqrt(lax.optimization_barrier(jnp.sum(image * image, axis=1, keepdims=True)))
    scale = lax.optimization_barrier(jnp.sum(vector * image, axis=1)) / lax.optimization_barrier(jnp.sum(vector * vector, axis=1))
    start = factor / scale[:, None, None]
    start_low = lowered(start)
    first_low = lowered((3.0 * identity - start) / 2.0)
    square_low = lowered(batched(first_low, first_low))
    moved = batched(square_low, start_low)
    second_low = lowered((3.0 * identity - moved) / 2.0)
    roots = lowered(batched(first_low, second_low) / jnp.sqrt(scale)[:, None, None])
    whitened = lowered(jnp.einsum('tkj,kjc->tkc', wide, roots.astype(jnp.float32), precision=HIGH))
    acts_flat = whitened[:, :half, :].reshape(tokens, half * block).astype(jnp.float32)
    grads_low = whitened[:, half:, :].astype(jnp.float32)
    update = jnp.einsum('ta,tbc->abc', acts_flat, grads_low, precision=HIGH) / math.sqrt(tokens)
    grads_flat = out_grads.reshape(tokens, half * block).astype(jnp.float32)
    input_grad = jnp.einsum('tj,bcj->tbc', grads_flat, weight.astype(jnp.float32), precision=HIGH)
    return (update.astype(jnp.bfloat16), input_grad.astype(jnp.bfloat16))
```

```python
import math

import jax
import jax.numpy as jnp
from jax import lax
from jax.sharding import Mesh
from jax.sharding import PartitionSpec as P

DAMPING = 0.1
COLUMNS = 64
SIDE_AT = (3, 0, 0, 2, 2, 1, 1, 3)
F32 = jnp.float32
BF16 = jnp.bfloat16


def split2(value):
    high = value.astype(BF16)
    low = (value - high.astype(F32)).astype(BF16)
    return high, low


def split3(value):
    high = value.astype(BF16)
    rest = value - high.astype(F32)
    middle = rest.astype(BF16)
    low = (rest - middle.astype(F32)).astype(BF16)
    return high, middle, low


def packed(rows, probe):
    return jnp.concatenate([*split2(rows), *split3(probe)], axis=0)


def unpacked(product):
    rows = product[:COLUMNS] + product[COLUMNS : 2 * COLUMNS]
    probe = product[2 * COLUMNS :]
    return rows, probe[0:1] + probe[1:2] + probe[2:3]


def by_tokens(rows, side):
    return jnp.einsum("nf,tf->nt", rows, side, preferred_element_type=F32)


def by_features(rows, side):
    return jnp.einsum("nt,tf->nf", rows, side, preferred_element_type=F32)


def whitened_columns(side, first, second):
    tokens, block = side.shape
    half = COLUMNS // 2
    row = lax.broadcasted_iota(jnp.int32, (COLUMNS, block), 0)
    wanted = jnp.where(row < half, first + row, second + row - half)
    unit = jnp.where(lax.broadcasted_iota(jnp.int32, (COLUMNS, block), 1) == wanted, 1.0, 0.0)

    def applied(rows, probe):
        return unpacked(by_tokens(packed(rows, probe), side))

    def back(rows, probe, z_rows, z_probe):
        f_rows, f_probe = unpacked(by_features(packed(z_rows, z_probe), side))
        return f_rows / tokens + DAMPING * rows, f_probe / tokens + DAMPING * probe

    ones = jnp.ones((1, block), F32)
    f1, u1 = back(unit, ones, *applied(unit, ones))
    f2, u2 = back(f1, u1, *applied(f1, u1))
    z2, zu = applied(f2, u2)
    norm = jnp.sum(u2 * u2)
    scale = (jnp.sum(zu * zu) / tokens + DAMPING * norm) / norm
    a1 = f1 / scale
    a2 = f2 / (scale * scale)
    f3 = by_features(jnp.concatenate(split2(z2), axis=0), side)
    f3 = (f3[:COLUMNS] + f3[COLUMNS:]) / tokens + DAMPING * f2
    a3 = f3 / (scale * scale * scale)

    def once(rows):
        z = by_tokens(jnp.concatenate(split2(rows), axis=0), side)
        return z[:COLUMNS] + z[COLUMNS:]

    f4 = by_features(jnp.concatenate(split2(once(a3)), axis=0), side)
    a4 = ((f4[:COLUMNS] + f4[COLUMNS:]) / tokens + DAMPING * a3) / scale
    root = (36.0 * unit - 39.0 * a1 + 27.0 * a2 - 9.0 * a3 + a4) / (16.0 * jnp.sqrt(scale))
    return once(root).astype(BF16)


def local(activations, out_grads, weight):
    tok_dev, blocks, width = activations.shape
    outs = lax.axis_size(("yl", "x", "c"))
    block = width * outs
    z, yl, x, c, yh = (lax.axis_index(a) for a in ("z", "yl", "x", "c", "yh"))
    token_count = tok_dev * lax.axis_size("z") * lax.axis_size("yh")

    pieces = [activations[:, 0], activations[:, 1], out_grads[:, 0], out_grads[:, 1]]
    mine = lax.all_to_all(jnp.stack([pieces[k] for k in SIDE_AT]), "z", 0, 0, tiled=True)
    mine = mine.reshape(8 * tok_dev, width)
    parts = lax.all_gather(mine, ("yl", "x", "c", "yh"), axis=0, tiled=False)
    side = parts.reshape(outs, 2, 8 * tok_dev, width).transpose(1, 2, 0, 3).reshape(token_count, block)

    is_act = jnp.logical_or(z % 4 == 1, z % 4 == 2)
    sub = (x * 2 + c) * 32
    act_first = ((z % 4) * 2 + yh) * 256 + sub
    act_second = (((z ^ 1) % 4) * 2 + yh) * 256 + sub
    upper = jnp.logical_or(z == 4, z == 0).astype(jnp.int32)
    grad_first = ((yl * 4 + x) * 2 + c) * width + upper * COLUMNS
    first = jnp.where(is_act, act_first, grad_first)
    second = jnp.where(is_act, act_second, grad_first + 32)
    done = whitened_columns(side, first, second)

    sent = lax.ppermute(done[32:], "z", [(1, 0), (2, 3), (5, 4), (6, 7)])
    act_part = jnp.where(is_act, done[:32], sent)
    acts = lax.all_gather(act_part, ("x", "c"), axis=0, tiled=True)
    got = {m: lax.ppermute(done, "z", [(s, s ^ m) for s in (0, 3, 4, 7)]) for m in range(1, 8)}
    slots = [jnp.where(is_act, got[m ^ 1], done if m == 0 else got[m]) for m in (0, 3, 4, 7)]
    tiles = [
        jnp.einsum("at,bt->ab", acts, slot, preferred_element_type=F32) / math.sqrt(token_count)
        for slot in slots
    ]
    base = jnp.where(is_act, z ^ 1, z)
    low_bit = base % 4 == 3
    high_bit = base >= 4
    t0, t3, t4, t7 = tiles
    t0, t3, t4, t7 = (jnp.where(low_bit, b, a) for a, b in ((t0, t3), (t3, t0), (t4, t7), (t7, t4)))
    t0, t3, t4, t7 = (jnp.where(high_bit, b, a) for a, b in ((t0, t4), (t3, t7), (t4, t0), (t7, t3)))
    update = jnp.stack(
        [jnp.concatenate([t3, t4], axis=1), jnp.concatenate([t7, t0], axis=1)], axis=1
    ).astype(BF16)

    grads_whole = lax.all_gather(out_grads, ("yl", "x", "c"), axis=2, tiled=True)
    input_grad = jnp.einsum(
        "tjq,bcjq->tbc",
        grads_whole,
        weight.reshape(blocks, width, blocks, block),
        preferred_element_type=F32,
    ).astype(BF16)
    return update, input_grad


def solution(mesh):
    split = Mesh(
        mesh.devices.reshape(mesh.shape["tok"], 2, 4, 2, mesh.shape["grp"]),
        ("z", "yl", "x", "c", "yh"),
    )
    out = ("yl", "x", "c")
    in_specs = (P(("z", "yh"), None, out), P(("z", "yh"), None, out), P(None, out, None))
    out_specs = (P(("z", "yh"), None, out), P(("z", "yh"), None, out))
    return jax.shard_map(local, mesh=split, in_specs=in_specs, out_specs=out_specs, check_vma=False)
```

```python
import math

import jax
import jax.numpy as jnp
from jax import lax
from jax.experimental import pallas as pl
from jax.experimental.pallas import tpu as pltpu
from jax.sharding import Mesh
from jax.sharding import PartitionSpec as P

DAMPING = 0.1
COLUMNS = 64
TILE = 512
SIDE_AT = (3, 0, 0, 2, 2, 1, 1, 3)
F32 = jnp.float32
BF16 = jnp.bfloat16


def split2(value):
    high = value.astype(BF16)
    low = (value - high.astype(F32)).astype(BF16)
    return high, low


def split3(value):
    high = value.astype(BF16)
    rest = value - high.astype(F32)
    middle = rest.astype(BF16)
    low = (rest - middle.astype(F32)).astype(BF16)
    return high, middle, low


def chain_kernel(*refs):
    where, pieces = refs[0], refs[1:17]
    out, side, turned, now, later, unit, f1, f2, a3, u1, u2, zu, sems = refs[17:]
    block, tokens = turned.shape
    half = COLUMNS // 2
    copies = []
    for at, (source, spot) in enumerate(placed(pieces)):
        row, col = spot
        to = side.at[row : row + 512, col : col + 128]
        copies.append((pltpu.make_async_copy(source, to, sems.at[at]), row, col))
        copies[-1][0].start()

    row_id = lax.broadcasted_iota(jnp.int32, (COLUMNS, block), 0)
    wanted = jnp.where(row_id < half, where[0] + row_id, where[1] + row_id - half)
    col_id = lax.broadcasted_iota(jnp.int32, (COLUMNS, block), 1)
    unit[...] = jnp.where(col_id == wanted, 1.0, 0.0)
    now[...] = jnp.zeros_like(now)
    now[:COLUMNS] = unit[...].astype(BF16)
    now[2 * COLUMNS : 2 * COLUMNS + 16] = jnp.where(
        lax.broadcasted_iota(jnp.int32, (16, block), 0) == 0, 1.0, 0.0
    ).astype(BF16)
    later[...] = jnp.zeros_like(later)
    for copy, row, col in copies:
        copy.wait()
        turned[col : col + 128, row : row + 512] = side[row : row + 512, col : col + 128].T

    def sweep(source, matrix, use):
        def tile(at, carry):
            cols = pl.ds(pl.multiple_of(at * TILE, TILE), TILE)
            product = jnp.dot(source[...], matrix[:, cols], preferred_element_type=F32)
            rows = product[:COLUMNS] + product[COLUMNS : 2 * COLUMNS]
            probe = product[2 * COLUMNS : 2 * COLUMNS + 1]
            probe += product[2 * COLUMNS + 1 : 2 * COLUMNS + 2]
            probe += product[2 * COLUMNS + 2 : 2 * COLUMNS + 3]
            use(at, cols, rows, probe)
            return carry

        lax.fori_loop(0, matrix.shape[1] // TILE, tile, 0)

    def keep(target, cols, rows, probe=None):
        target[:COLUMNS, cols], target[COLUMNS : 2 * COLUMNS, cols] = split2(rows)
        if probe is not None:
            high, middle, low = split3(probe)
            at = lax.broadcasted_iota(jnp.int32, (16, TILE), 0)
            stacked = jnp.where(at == 0, high.astype(F32), jnp.where(at == 1, middle.astype(F32), low.astype(F32)))
            target[2 * COLUMNS : 2 * COLUMNS + 16, cols] = jnp.where(at < 3, stacked, 0.0).astype(BF16)

    def to_later(_, cols, rows, probe):
        keep(later, cols, rows, probe)

    def first_power(_, cols, rows, probe):
        rows = rows / tokens + DAMPING * unit[:, cols]
        probe = probe / tokens + DAMPING
        f1[:, cols], u1[:, cols] = rows, probe
        keep(now, cols, rows, probe)

    def second_power(_, cols, rows, probe):
        rows = rows / tokens + DAMPING * f1[:, cols]
        probe = probe / tokens + DAMPING * u1[:, cols]
        f2[:, cols], u2[:, cols] = rows, probe
        keep(now, cols, rows, probe)

    def rayleigh(_, cols, rows, probe):
        keep(later, cols, rows)
        zu[:, cols] = probe

    sweep(now, turned, to_later)
    sweep(later, side, first_power)
    sweep(now, turned, to_later)
    sweep(later, side, second_power)
    sweep(now, turned, rayleigh)
    norm = jnp.sum(u2[...] * u2[...], axis=1, keepdims=True)
    scale = (jnp.sum(zu[...] * zu[...], axis=1, keepdims=True) / tokens + DAMPING * norm) / norm
    inverse = 1.0 / scale
    inverse2 = inverse * inverse
    final = 1.0 / (16.0 * jnp.sqrt(scale))

    def third_power(_, cols, rows, probe):
        rows = (rows / tokens + DAMPING * f2[:, cols]) * (inverse2 * inverse)
        a3[:, cols] = rows
        keep(now, cols, rows)

    def root(_, cols, rows, probe):
        a4 = (rows / tokens + DAMPING * a3[:, cols]) * inverse
        rows = 36.0 * unit[:, cols] - 39.0 * (f1[:, cols] * inverse) + 27.0 * (f2[:, cols] * inverse2)
        rows = (rows - 9.0 * a3[:, cols] + a4) * final
        keep(now, cols, rows)

    def result(at, cols, rows, probe):
        spot = (at + where[2] * (tokens // TILE // 2)) % (tokens // TILE)
        out[:, pl.ds(pl.multiple_of(spot * TILE, TILE), TILE)] = rows.astype(BF16)

    sweep(later, side, third_power)
    sweep(now, turned, lambda _, cols, rows, probe: keep(later, cols, rows))
    sweep(later, side, root)
    sweep(now, turned, result)


def placed(pieces):
    for core in range(2):
        for at in range(4):
            by_y, by_x = pieces[core * 8 + at], pieces[core * 8 + 4 + at]
            for inner in range(4):
                part = pl.ds(inner * 512, 512)
                yield by_y.at[part], (at // 2 * 1024, ((at % 2) * 8 + inner * 2 + core) * 128)
                yield by_x.at[part], (inner // 2 * 1024 + 512, ((inner % 2) * 8 + at * 2 + core) * 128)


def whitened_columns(pieces, where, block, tokens):
    rows = 2 * COLUMNS + 16
    passes = 9 * 2 * rows * block * tokens
    return pl.pallas_call(
        chain_kernel,
        name="whiten",
        out_shape=jax.ShapeDtypeStruct((COLUMNS, tokens), BF16),
        in_specs=[pl.BlockSpec(memory_space=pltpu.SMEM)] + [pl.BlockSpec(memory_space=pl.ANY)] * 16,
        out_specs=pl.BlockSpec(memory_space=pltpu.VMEM),
        scratch_shapes=[
            pltpu.VMEM((tokens, block), BF16),
            pltpu.VMEM((block, tokens), BF16),
            pltpu.VMEM((rows, block), BF16),
            pltpu.VMEM((rows, tokens), BF16),
            *[pltpu.VMEM((COLUMNS, block), F32)] * 4,
            *[pltpu.VMEM((1, block), F32)] * 3,
            pltpu.SemaphoreType.DMA((64,)),
        ],
        compiler_params=pltpu.CompilerParams(vmem_limit_bytes=32 * 2**20),
        cost_estimate=pl.CostEstimate(flops=passes, bytes_accessed=2 * block * tokens, transcendentals=0),
    )(where, *pieces)


def xor_swap(array, axes, mask, order=lambda i: i, back=lambda i: i):
    count = lax.axis_size(axes)
    return lax.ppermute(array, axes, [(i, back(order(i) ^ mask)) for i in range(count)])


def y_of(i):
    return i % 2 * 2 + i // 2


def side_pieces(mine):
    lower, upper = mine[:512], mine[512:]
    masks = (1, 3, 2)
    lower_x, upper_y = {0: lower}, {0: upper}
    for m in masks:
        lower_x[m] = xor_swap(lower, "x", m)
        upper_y[m] = xor_swap(upper, ("yl", "yh"), m, y_of, y_of)
    by_y = {0: jnp.concatenate([lower_x[m] for m in range(4)])}
    by_x = {0: jnp.concatenate([upper_y[m] for m in range(4)])}
    for m in masks:
        by_y[m] = xor_swap(by_y[0], ("yl", "yh"), m, y_of, y_of)
        by_x[m] = xor_swap(by_x[0], "x", m)
    own = [by_y[m] for m in range(4)] + [by_x[m] for m in range(4)]
    return own + [xor_swap(piece, "c", 1) for piece in own]


def local(activations, out_grads, weight):
    tok_dev, blocks, width = activations.shape
    outs = lax.axis_size(("yl", "x", "c"))
    block = width * outs
    z, yl, x, c, yh = (lax.axis_index(a) for a in ("z", "yl", "x", "c", "yh"))
    token_count = tok_dev * lax.axis_size("z") * lax.axis_size("yh")

    pieces = [activations[:, 0], activations[:, 1], out_grads[:, 0], out_grads[:, 1]]
    mine = lax.all_to_all(jnp.stack([pieces[k] for k in SIDE_AT]), "z", 0, 0, tiled=True)
    mine = mine.reshape(8 * tok_dev, width)
    pieces = side_pieces(mine)

    is_act = jnp.logical_or(z % 4 == 1, z % 4 == 2)
    sub = (x * 2 + c) * 32
    act_first = ((z % 4) * 2 + yh) * 256 + sub
    act_second = (((z ^ 1) % 4) * 2 + yh) * 256 + sub
    upper = jnp.logical_or(z == 4, z == 0).astype(jnp.int32)

    def relative(column):
        place = column // width
        return (((place // 8) ^ yl) * 8 + ((place // 2 % 4) ^ x) * 2 + ((place % 2) ^ c)) * width + column % width

    first = jnp.where(is_act, relative(act_first), upper * COLUMNS)
    second = jnp.where(is_act, relative(act_second), upper * COLUMNS + 32)
    done = whitened_columns(pieces, jnp.stack([first, second, yh]), block, token_count)

    sent = lax.ppermute(done[32:], "z", [(1, 0), (2, 3), (5, 4), (6, 7)])
    act_part = jnp.where(is_act, done[:32], sent)
    acts = lax.all_gather(act_part, ("x", "c"), axis=0, tiled=True)
    got = {m: lax.ppermute(done, "z", [(s, s ^ m) for s in (0, 3, 4, 7)]) for m in range(1, 8)}
    slots = [jnp.where(is_act, got[m ^ 1], done if m == 0 else got[m]) for m in (0, 3, 4, 7)]
    tiles = [
        jnp.einsum("at,bt->ab", acts, slot, preferred_element_type=F32) / math.sqrt(token_count)
        for slot in slots
    ]
    base = jnp.where(is_act, z ^ 1, z)
    low_bit = base % 4 == 3
    high_bit = base >= 4
    t0, t3, t4, t7 = tiles
    t0, t3, t4, t7 = (jnp.where(low_bit, b, a) for a, b in ((t0, t3), (t3, t0), (t4, t7), (t7, t4)))
    t0, t3, t4, t7 = (jnp.where(high_bit, b, a) for a, b in ((t0, t4), (t3, t7), (t4, t0), (t7, t3)))
    update = jnp.stack(
        [jnp.concatenate([t3, t4], axis=1), jnp.concatenate([t7, t0], axis=1)], axis=1
    ).astype(BF16)

    late_grads, _ = lax.optimization_barrier((out_grads, pieces[4]))
    grads_whole = lax.all_gather(late_grads, ("yl", "x", "c"), axis=2, tiled=True)
    input_grad = jnp.einsum(
        "tjq,bcjq->tbc",
        grads_whole,
        weight.reshape(blocks, width, blocks, block),
        preferred_element_type=F32,
    ).astype(BF16)
    return update, input_grad


def solution(mesh):
    split = Mesh(
        mesh.devices.reshape(mesh.shape["tok"], 2, 4, 2, mesh.shape["grp"]),
        ("z", "yl", "x", "c", "yh"),
    )
    out = ("yl", "x", "c")
    in_specs = (P(("z", "yh"), None, out), P(("z", "yh"), None, out), P(None, out, None))
    out_specs = (P(("z", "yh"), None, out), P(("z", "yh"), None, out))
    return jax.shard_map(local, mesh=split, in_specs=in_specs, out_specs=out_specs, check_vma=False)
```

```python
import math

import jax
import jax.numpy as jnp
from jax import lax
from jax.experimental import pallas as pl
from jax.experimental.pallas import tpu as pltpu
from jax.sharding import Mesh
from jax.sharding import PartitionSpec as P

DAMPING = 0.1
COLUMNS = 64
TILE = 512
SIDE_AT = (3, 0, 0, 2, 2, 1, 1, 3)
F32 = jnp.float32
BF16 = jnp.bfloat16


def split2(value):
    high = value.astype(BF16)
    low = (value - high.astype(F32)).astype(BF16)
    return high, low


def split3(value):
    high = value.astype(BF16)
    rest = value - high.astype(F32)
    middle = rest.astype(BF16)
    low = (rest - middle.astype(F32)).astype(BF16)
    return high, middle, low


def chain_kernel(*refs):
    where, pieces = refs[0], refs[1:9]
    out, side, turned, now, later, unit, f1, f2, a3, u1, u2, zu, sems = refs[9:]
    block, tokens = turned.shape
    half = COLUMNS // 2
    copies = []
    for source, row, col in placed(pieces, where[3] == 0):
        row, col = pl.multiple_of(row, 512), pl.multiple_of(col, 128)
        to = side.at[pl.ds(row, 512), pl.ds(col, 128)]
        copies.append((pltpu.make_async_copy(source, to, sems.at[len(copies)]), row, col))
        copies[-1][0].start()

    row_id = lax.broadcasted_iota(jnp.int32, (COLUMNS, block), 0)
    wanted = jnp.where(row_id < half, where[0] + row_id, where[1] + row_id - half)
    col_id = lax.broadcasted_iota(jnp.int32, (COLUMNS, block), 1)
    unit[...] = jnp.where(col_id == wanted, 1.0, 0.0)
    now[...] = jnp.zeros_like(now)
    now[:COLUMNS] = unit[...].astype(BF16)
    now[2 * COLUMNS : 2 * COLUMNS + 16] = jnp.where(
        lax.broadcasted_iota(jnp.int32, (16, block), 0) == 0, 1.0, 0.0
    ).astype(BF16)
    later[...] = jnp.zeros_like(later)
    for copy, row, col in copies:
        copy.wait()
        turned[pl.ds(col, 128), pl.ds(row, 512)] = side[pl.ds(row, 512), pl.ds(col, 128)].T

    def sweep(source, matrix, use):
        def tile(at, carry):
            cols = pl.ds(pl.multiple_of(at * TILE, TILE), TILE)
            product = jnp.dot(source[...], matrix[:, cols], preferred_element_type=F32)
            rows = product[:COLUMNS] + product[COLUMNS : 2 * COLUMNS]
            probe = product[2 * COLUMNS : 2 * COLUMNS + 1]
            probe += product[2 * COLUMNS + 1 : 2 * COLUMNS + 2]
            probe += product[2 * COLUMNS + 2 : 2 * COLUMNS + 3]
            use(at, cols, rows, probe)
            return carry

        lax.fori_loop(0, matrix.shape[1] // TILE, tile, 0)

    def keep(target, cols, rows, probe=None):
        target[:COLUMNS, cols], target[COLUMNS : 2 * COLUMNS, cols] = split2(rows)
        if probe is not None:
            high, middle, low = split3(probe)
            at = lax.broadcasted_iota(jnp.int32, (16, TILE), 0)
            stacked = jnp.where(at == 0, high.astype(F32), jnp.where(at == 1, middle.astype(F32), low.astype(F32)))
            target[2 * COLUMNS : 2 * COLUMNS + 16, cols] = jnp.where(at < 3, stacked, 0.0).astype(BF16)

    def to_later(_, cols, rows, probe):
        keep(later, cols, rows, probe)

    def first_power(_, cols, rows, probe):
        rows = rows / tokens + DAMPING * unit[:, cols]
        probe = probe / tokens + DAMPING
        f1[:, cols], u1[:, cols] = rows, probe
        keep(now, cols, rows, probe)

    def second_power(_, cols, rows, probe):
        rows = rows / tokens + DAMPING * f1[:, cols]
        probe = probe / tokens + DAMPING * u1[:, cols]
        f2[:, cols], u2[:, cols] = rows, probe
        keep(now, cols, rows, probe)

    def rayleigh(_, cols, rows, probe):
        keep(later, cols, rows)
        zu[:, cols] = probe

    sweep(now, turned, to_later)
    sweep(later, side, first_power)
    sweep(now, turned, to_later)
    sweep(later, side, second_power)
    sweep(now, turned, rayleigh)
    norm = jnp.sum(u2[...] * u2[...], axis=1, keepdims=True)
    scale = (jnp.sum(zu[...] * zu[...], axis=1, keepdims=True) / tokens + DAMPING * norm) / norm
    inverse = 1.0 / scale
    inverse2 = inverse * inverse
    final = 1.0 / (16.0 * jnp.sqrt(scale))

    def third_power(_, cols, rows, probe):
        rows = (rows / tokens + DAMPING * f2[:, cols]) * (inverse2 * inverse)
        a3[:, cols] = rows
        keep(now, cols, rows)

    def root(_, cols, rows, probe):
        a4 = (rows / tokens + DAMPING * a3[:, cols]) * inverse
        rows = 36.0 * unit[:, cols] - 39.0 * (f1[:, cols] * inverse) + 27.0 * (f2[:, cols] * inverse2)
        rows = (rows - 9.0 * a3[:, cols] + a4) * final
        keep(now, cols, rows)

    def result(at, cols, rows, probe):
        spot = at ^ where[2]
        out[:, pl.ds(pl.multiple_of(spot * TILE, TILE), TILE)] = rows.astype(BF16)

    sweep(later, side, third_power)
    sweep(now, turned, lambda _, cols, rows, probe: keep(later, cols, rows))
    sweep(later, side, root)
    sweep(now, turned, result)


def placed(pieces, first_core):
    for core in range(2):
        for outer in range(4):
            for inner in range(4):
                for other in range(2):
                    part = pieces[core * 4 + outer].at[pl.ds((inner * 2 + other) * 512, 512)]

                    def spot(x, y):
                        return y // 2 * 1024 + core * 512, (y % 2 * 8 + x * 2 + (core ^ other)) * 128

                    x_first, y_first = spot(inner, outer), spot(outer, inner)
                    if core:
                        x_first, y_first = y_first, x_first
                    yield part, *(jnp.where(first_core, p, q) for p, q in zip(x_first, y_first))


def whitened_columns(pieces, where, block, tokens):
    rows = 2 * COLUMNS + 16
    passes = 9 * 2 * rows * block * tokens
    return pl.pallas_call(
        chain_kernel,
        name="whiten",
        out_shape=jax.ShapeDtypeStruct((COLUMNS, tokens), BF16),
        in_specs=[pl.BlockSpec(memory_space=pltpu.SMEM)] + [pl.BlockSpec(memory_space=pl.ANY)] * 8,
        out_specs=pl.BlockSpec(memory_space=pltpu.VMEM),
        scratch_shapes=[
            pltpu.VMEM((tokens, block), BF16),
            pltpu.VMEM((block, tokens), BF16),
            pltpu.VMEM((rows, block), BF16),
            pltpu.VMEM((rows, tokens), BF16),
            *[pltpu.VMEM((COLUMNS, block), F32)] * 4,
            *[pltpu.VMEM((1, block), F32)] * 3,
            pltpu.SemaphoreType.DMA((64,)),
        ],
        compiler_params=pltpu.CompilerParams(vmem_limit_bytes=32 * 2**20),
        cost_estimate=pl.CostEstimate(flops=passes, bytes_accessed=2 * block * tokens, transcendentals=0),
    )(where, *pieces)


def xor_swap(array, axis, mask):
    return lax.ppermute(array, axis, [(i, i ^ mask) for i in range(lax.axis_size(axis))])


def plane_swap(array, first_mask, second_mask):
    def at(x, y, c):
        return (((y % 2) * 4 + x) * 2 + c) * 2 + y // 2

    pairs = []
    for x in range(4):
        for y in range(4):
            pairs.append((at(x, y, 0), at(x ^ first_mask, y ^ second_mask, 0)))
            pairs.append((at(x, y, 1), at(x ^ second_mask, y ^ first_mask, 1)))
    return lax.ppermute(array, ("yl", "x", "c", "yh"), pairs)


def side_pieces(mine, c):
    lower, upper = mine[:512], mine[512:]
    keep, give = jnp.where(c == 0, lower, upper), jnp.where(c == 0, upper, lower)
    part = jnp.concatenate([keep, xor_swap(give, "c", 1)])
    masks = (1, 3, 2)
    step = {0: part, **{m: plane_swap(part, m, 0) for m in masks}}
    row = jnp.concatenate([step[m] for m in range(4)])
    wide = {0: row, **{m: plane_swap(row, 0, m) for m in masks}}
    own = [wide[m] for m in range(4)]
    return own + [xor_swap(piece, "c", 1) for piece in own]


def tile_kernel(where, own, other, *refs):
    parts, out, grads = refs[:8], refs[8], refs[9]
    tokens = grads.shape[1]
    for slot in range(4):
        chosen = jnp.where(where[0] == 1, parts[2 * slot + 1][...], parts[2 * slot][...])
        grads[pl.ds(pl.multiple_of(where[2 + slot] * COLUMNS, COLUMNS), COLUMNS), :] = chosen
    for core, acts in enumerate((own, other)):
        product = lax.dot_general(
            acts[...], grads[...], (((1,), (1,)), ((), ())), preferred_element_type=F32
        )
        product = (product / math.sqrt(tokens)).astype(BF16)
        for at in range(4):
            row = pl.multiple_of(((at * 2 + core) ^ where[1]) * 32, 32)
            for side in range(2):
                out[side, pl.ds(row, 32), :] = product[at * 32 : at * 32 + 32, side * 128 : side * 128 + 128]


def update_tile(where, own, other, parts):
    tokens = own.shape[1]
    return pl.pallas_call(
        tile_kernel,
        name="update_tile",
        out_shape=jax.ShapeDtypeStruct((2, 256, 128), BF16),
        in_specs=[pl.BlockSpec(memory_space=pltpu.SMEM)] + [pl.BlockSpec(memory_space=pltpu.VMEM)] * 10,
        out_specs=pl.BlockSpec(memory_space=pltpu.VMEM),
        scratch_shapes=[pltpu.VMEM((4 * COLUMNS, tokens), BF16)],
        compiler_params=pltpu.CompilerParams(vmem_limit_bytes=16 * 2**20),
        cost_estimate=pl.CostEstimate(flops=2 * 256 * 256 * tokens, bytes_accessed=3 * 2**20, transcendentals=0),
    )(where, own, other, *parts)


def local(activations, out_grads, weight):
    tok_dev, blocks, width = activations.shape
    outs = lax.axis_size(("yl", "x", "c"))
    block = width * outs
    z, yl, x, c, yh = (lax.axis_index(a) for a in ("z", "yl", "x", "c", "yh"))
    token_count = tok_dev * lax.axis_size("z") * lax.axis_size("yh")

    pieces = [activations[:, 0], activations[:, 1], out_grads[:, 0], out_grads[:, 1]]
    mine = lax.all_to_all(jnp.stack([pieces[k] for k in SIDE_AT]), "z", 0, 0, tiled=True)
    mine = mine.reshape(8 * tok_dev, width)
    pieces = side_pieces(mine, c)

    is_act = jnp.logical_or(z % 4 == 1, z % 4 == 2)
    sub = (x * 2 + c) * 32
    act_first = ((z % 4) * 2 + yh) * 256 + sub
    act_second = (((z ^ 1) % 4) * 2 + yh) * 256 + sub
    upper = jnp.logical_or(z == 4, z == 0).astype(jnp.int32)

    def relative(column):
        place = column // width
        return (((place // 8) ^ yl) * 8 + ((place // 2 % 4) ^ x) * 2 + ((place % 2) ^ c)) * width + column % width

    first = jnp.where(is_act, relative(act_first), upper * COLUMNS)
    second = jnp.where(is_act, relative(act_second), upper * COLUMNS + 32)
    done = whitened_columns(pieces, jnp.stack([first, second, yh * 2 + c, c]), block, token_count)

    sent = lax.ppermute(done[32:], "z", [(1, 0), (2, 3), (5, 4), (6, 7)])
    act_part = jnp.where(is_act, done[:32], sent)
    got = {m: lax.ppermute(done, "z", [(s, s ^ m) for s in (0, 3, 4, 7)]) for m in range(1, 8)}
    acts = {0: act_part, **{m: xor_swap(act_part, "x", m) for m in (1, 3, 2)}}
    acts = jnp.concatenate([acts[m] for m in range(4)])
    base = jnp.where(is_act, z ^ 1, z)
    spots = []
    for m in (0, 3, 4, 7):
        at = base ^ m
        spots.append(jnp.where(at == 3, 0, jnp.where(at == 4, 1, jnp.where(at == 7, 2, 3))))
    parts = [part for m in (0, 3, 4, 7) for part in (got[m] if m else done, got[m ^ 1])]
    numbers = jnp.stack([is_act.astype(jnp.int32), x * 2 + c, *spots]).astype(jnp.int32)
    update = update_tile(numbers, acts, xor_swap(acts, "c", 1), parts).transpose(1, 0, 2)

    late_grads, _ = lax.optimization_barrier((out_grads, pieces[4]))
    grads_whole = lax.all_gather(late_grads, ("yl", "x", "c"), axis=2, tiled=True)
    input_grad = jnp.einsum(
        "tjq,bcjq->tbc",
        grads_whole,
        weight.reshape(blocks, width, blocks, block),
        preferred_element_type=F32,
    ).astype(BF16)
    return update, input_grad


def solution(mesh):
    split = Mesh(
        mesh.devices.reshape(mesh.shape["tok"], 2, 4, 2, mesh.shape["grp"]),
        ("z", "yl", "x", "c", "yh"),
    )
    out = ("yl", "x", "c")
    in_specs = (P(("z", "yh"), None, out), P(("z", "yh"), None, out), P(None, out, None))
    out_specs = (P(("z", "yh"), None, out), P(("z", "yh"), None, out))
    return jax.shard_map(local, mesh=split, in_specs=in_specs, out_specs=out_specs, check_vma=False)
```

```python
import math

import jax
import jax.numpy as jnp
from jax import lax
from jax.experimental import pallas as pl
from jax.experimental.pallas import tpu as pltpu
from jax.sharding import Mesh
from jax.sharding import PartitionSpec as P

DAMPING = 0.1
COLUMNS = 64
GRADS_AT = (0, 3, 4, 7)
F32 = jnp.float32
BF16 = jnp.bfloat16


def split2(value):
    high = value.astype(BF16)
    low = (value - high.astype(F32)).astype(BF16)
    return high, low


def split3(value):
    high = value.astype(BF16)
    rest = value - high.astype(F32)
    middle = rest.astype(BF16)
    low = (rest - middle.astype(F32)).astype(BF16)
    return high, middle, low


def chain_kernel(where, *refs):
    pieces = refs[:8]
    out, side, turned, now, later, f1, f2, f3, u1, u2, sems = refs[8:]
    block, tokens = turned.shape
    half = COLUMNS // 2
    copies = []
    for source, row, col in placed(pieces, where[3] == 0, where[4]):
        row, col = pl.multiple_of(row, 512), pl.multiple_of(col, 128)
        to = side.at[pl.ds(row, 512), pl.ds(col, 128)]
        copies.append((pltpu.make_async_copy(source, to, sems.at[len(copies)]), row, col))
        copies[-1][0].start()
    now[...] = jnp.zeros_like(now)
    later[...] = jnp.zeros_like(later)
    for copy, row, col in copies:
        copy.wait()
        turned[pl.ds(col, 128), pl.ds(row, 512)] = side[pl.ds(row, 512), pl.ds(col, 128)].T

    probe_at = pl.ds(2 * COLUMNS, 16)
    probe_row = lax.broadcasted_iota(jnp.int32, (16, block), 0)

    def times(rows, matrix):
        product = jnp.dot(rows[...], matrix[...], preferred_element_type=F32)
        probe = jnp.sum(product[2 * COLUMNS :], axis=0, keepdims=True)
        return product[:COLUMNS] + product[COLUMNS : 2 * COLUMNS], probe

    def keep(target, rows, probe=None):
        target[:COLUMNS], target[COLUMNS : 2 * COLUMNS] = split2(rows)
        if probe is not None:
            high, middle, low = (part.astype(F32) for part in split3(probe))
            stacked = jnp.where(probe_row == 0, high, jnp.where(probe_row == 1, middle, low))
            target[probe_at] = jnp.where(probe_row < 3, stacked, 0.0).astype(BF16)

    def unit():
        row = lax.broadcasted_iota(jnp.int32, (COLUMNS, block), 0)
        wanted = jnp.where(row < half, where[0] + row, where[1] + row - half)
        col = lax.broadcasted_iota(jnp.int32, (COLUMNS, block), 1)
        return jnp.where(col == wanted, 1.0, 0.0)

    later[:half] = turned[pl.ds(pl.multiple_of(where[0], half), half), :]
    later[half:COLUMNS] = turned[pl.ds(pl.multiple_of(where[1], half), half), :]
    rows, _ = times(later, side)
    rows = rows / tokens + DAMPING * unit()
    f1[...] = rows
    keep(now, rows, jnp.ones((1, block), F32))
    keep(later, *times(now, turned))
    rows, probe = times(later, side)
    rows, probe = rows / tokens + DAMPING * f1[...], probe / tokens + DAMPING
    f2[...], u1[...] = rows, probe
    keep(now, rows, probe)
    keep(later, *times(now, turned))
    rows, probe = times(later, side)
    rows, probe = rows / tokens + DAMPING * f2[...], probe / tokens + DAMPING * u1[...]
    f3[...], u2[...] = rows, probe
    keep(now, rows, probe)
    rows, probe = times(now, turned)
    keep(later, rows)
    norm = jnp.sum(u2[...] * u2[...], axis=1, keepdims=True)
    scale = (jnp.sum(probe * probe, axis=1, keepdims=True) / tokens + DAMPING * norm) / norm
    inverse = 1.0 / scale
    inverse2 = inverse * inverse
    rows, _ = times(later, side)
    a3 = f3[...] * (inverse2 * inverse)
    a4 = (rows / tokens) * (inverse2 * inverse2) + DAMPING * (a3 * inverse)
    total = 36.0 * unit() - 39.0 * (f1[...] * inverse) + 27.0 * (f2[...] * inverse2)
    keep(now, (total - 9.0 * a3 + a4) * (1.0 / (16.0 * jnp.sqrt(scale))))
    rows, _ = times(now, turned)
    for at in range(tokens // 128):
        to = pl.ds(pl.multiple_of((at ^ where[2]) * 128, 128), 128)
        out[:, to] = rows[:, at * 128 : at * 128 + 128].astype(BF16)


def placed(pieces, first_core, upper_z):
    for core in range(2):
        for outer in range(4):
            for inner in range(4):
                for other in range(2):
                    part = pieces[core * 4 + outer].at[pl.ds((inner * 2 + other) * 512, 512)]

                    def spot(x, y):
                        return y // 2 * 1024 + core * 512, (y % 2 * 8 + x * 2) * 128

                    x_first, y_first = spot(inner, outer), spot(outer, inner)
                    if core:
                        x_first, y_first = y_first, x_first
                    row, col = (jnp.where(first_core, p, q) for p, q in zip(x_first, y_first))
                    yield part, row, col + ((core ^ other) ^ upper_z) * 128


def whitened_columns(pieces, where, block, tokens):
    rows = 2 * COLUMNS + 16
    passes = 8 * 2 * rows * block * tokens
    return pl.pallas_call(
        chain_kernel,
        name="whiten",
        out_shape=jax.ShapeDtypeStruct((COLUMNS, tokens), BF16),
        in_specs=[pl.BlockSpec(memory_space=pltpu.SMEM)] + [pl.BlockSpec(memory_space=pl.ANY)] * 8,
        out_specs=pl.BlockSpec(memory_space=pltpu.VMEM),
        scratch_shapes=[
            pltpu.VMEM((tokens, block), BF16),
            pltpu.VMEM((block, tokens), BF16),
            pltpu.VMEM((rows, block), BF16),
            pltpu.VMEM((rows, tokens), BF16),
            *[pltpu.VMEM((COLUMNS, block), F32)] * 3,
            *[pltpu.VMEM((1, block), F32)] * 2,
            pltpu.SemaphoreType.DMA((64,)),
        ],
        compiler_params=pltpu.CompilerParams(vmem_limit_bytes=32 * 2**20),
        cost_estimate=pl.CostEstimate(flops=passes, bytes_accessed=2 * block * tokens, transcendentals=0),
    )(where, *pieces)


def xor_swap(array, axis, mask):
    return lax.ppermute(array, axis, [(i, i ^ mask) for i in range(lax.axis_size(axis))])


def z_and_x_swap(array, mask, q):
    pairs = []
    for z in range(8):
        for x in range(4):
            if z not in GRADS_AT:
                pairs.append((z * 4 + x, (z if mask else z ^ 1) * 4 + (x ^ q)))
            elif mask:
                pairs.append((z * 4 + x, (z ^ mask) * 4 + x))
    return lax.ppermute(array, ("z", "x"), pairs)


def plane_swap(array, first_mask, second_mask):
    def at(x, y, c):
        return (((y % 2) * 4 + x) * 2 + c) * 2 + y // 2

    pairs = []
    for x in range(4):
        for y in range(4):
            pairs.append((at(x, y, 0), at(x ^ first_mask, y ^ second_mask, 0)))
            pairs.append((at(x, y, 1), at(x ^ second_mask, y ^ first_mask, 1)))
    return lax.ppermute(array, ("yl", "x", "c", "yh"), pairs)


def side_parts(activations, out_grads, z, c):
    acts_here = (z ^ z // 2) % 2 == 1
    same = jnp.where(acts_here, activations, out_grads)
    other = jnp.where(acts_here, out_grads, activations)
    swap = (z // 4) ^ c == 1
    pieces = [jnp.where(swap, kind[:, 1 - j], kind[:, j]) for kind in (same, other) for j in range(2)]
    parts = []
    for m in range(8):
        pairs = [(i * 2 + j, (i ^ m ^ (4 * j)) * 2 + i // 4) for i in range(8) for j in range(2)]
        parts.append(lax.ppermute(pieces[(m ^ m // 2) % 2 * 2 + m // 4], ("z", "c"), pairs))
    return parts


def side_pieces(parts):
    part = jnp.concatenate(parts)
    masks = (1, 3, 2)
    step = {0: part, **{m: plane_swap(part, m, 0) for m in masks}}
    row = jnp.concatenate([step[m] for m in range(4)])
    wide = {0: row, **{m: plane_swap(row, 0, m) for m in masks}}
    own = [wide[m] for m in range(4)]
    return own + [xor_swap(piece, "c", 1) for piece in own]


def tile_kernel(where, own, other, *refs):
    parts, out, grads = refs[:8], refs[8], refs[9]
    tokens = grads.shape[1]
    for slot in range(4):
        chosen = jnp.where(where[0] == 1, parts[2 * slot + 1][...], parts[2 * slot][...])
        grads[pl.ds(pl.multiple_of(where[2 + slot] * COLUMNS, COLUMNS), COLUMNS), :] = chosen
    for core, acts in enumerate((own, other)):
        product = lax.dot_general(
            acts[...], grads[...], (((1,), (1,)), ((), ())), preferred_element_type=F32
        )
        product = (product / math.sqrt(tokens)).astype(BF16)
        for at in range(4):
            row = pl.multiple_of(((at * 2 + core) ^ where[1]) * 32, 32)
            for side in range(2):
                out[side, pl.ds(row, 32), :] = product[at * 32 : at * 32 + 32, side * 128 : side * 128 + 128]


def update_tile(where, own, other, parts):
    tokens = own.shape[1]
    return pl.pallas_call(
        tile_kernel,
        name="update_tile",
        out_shape=jax.ShapeDtypeStruct((2, 256, 128), BF16),
        in_specs=[pl.BlockSpec(memory_space=pltpu.SMEM)] + [pl.BlockSpec(memory_space=pltpu.VMEM)] * 10,
        out_specs=pl.BlockSpec(memory_space=pltpu.VMEM),
        scratch_shapes=[pltpu.VMEM((4 * COLUMNS, tokens), BF16)],
        compiler_params=pltpu.CompilerParams(vmem_limit_bytes=16 * 2**20),
        cost_estimate=pl.CostEstimate(flops=2 * 256 * 256 * tokens, bytes_accessed=3 * 2**20, transcendentals=0),
    )(where, own, other, *parts)


def local(activations, out_grads, weight):
    tok_dev, blocks, width = activations.shape
    outs = lax.axis_size(("yl", "x", "c"))
    block = width * outs
    z, yl, x, c, yh = (lax.axis_index(a) for a in ("z", "yl", "x", "c", "yh"))
    token_count = tok_dev * lax.axis_size("z") * lax.axis_size("yh")

    pieces = side_pieces(side_parts(activations, out_grads, z, c))

    is_act = jnp.logical_or(z % 4 == 1, z % 4 == 2)
    sub = (x * 2 + c) * 32
    act_first = ((z % 4) * 2 + yh) * 256 + sub
    act_second = (((z ^ 1) % 4) * 2 + yh) * 256 + sub
    upper = z % 2

    def relative(column):
        place = column // width
        return (((place // 8) ^ yl) * 8 + ((place // 2 % 4) ^ x) * 2 + ((place % 2) ^ c)) * width + column % width

    first = jnp.where(is_act, relative(act_first), upper * COLUMNS)
    second = jnp.where(is_act, relative(act_second), upper * COLUMNS + 32)
    done = whitened_columns(pieces, jnp.stack([first, second, yh * 8 + c * 4 + z % 4, c, z // 4]), block, token_count)

    late_grads, _ = lax.optimization_barrier((out_grads, pieces[1]))
    grads_whole = lax.all_gather(late_grads, ("yl", "x", "c"), axis=2, tiled=True)
    input_grad = jnp.einsum(
        "tjq,bcjq->tbc",
        grads_whole,
        weight.reshape(blocks, width, blocks, block),
        preferred_element_type=F32,
    ).astype(BF16)

    near = {m: z_and_x_swap(done, m, q) for q, m in ((1, 3), (2, 7), (3, 4))}
    far = {q: z_and_x_swap(done[32:], None, q) for q in range(4)}
    got = {m: lax.ppermute(done, "z", [(s, s ^ m) for s in GRADS_AT]) for m in (1, 2, 5, 6)}
    acts = [jnp.where(is_act, done[:32], far[0])]
    acts += [jnp.where(is_act, near[m][:32], far[q]) for q, m in ((1, 3), (2, 7), (3, 4))]
    acts, input_grad = lax.optimization_barrier((jnp.concatenate(acts), input_grad))
    base = jnp.where(is_act, z ^ 1, z)
    spots = [(base ^ m) // 4 * 2 + (base ^ m) % 2 for m in GRADS_AT]
    parts = [part for m in GRADS_AT for part in (near[m] if m else done, got[m ^ 1])]
    numbers = jnp.stack([is_act.astype(jnp.int32), x * 2 + c, *spots]).astype(jnp.int32)
    update = update_tile(numbers, acts, xor_swap(acts, "c", 1), parts).transpose(1, 0, 2)
    return update, input_grad


def solution(mesh):
    split = Mesh(
        mesh.devices.reshape(mesh.shape["tok"], 2, 4, 2, mesh.shape["grp"]),
        ("z", "yl", "x", "c", "yh"),
    )
    out = ("yl", "x", "c")
    in_specs = (P(("z", "yh"), None, out), P(("z", "yh"), None, out), P(None, out, None))
    out_specs = (P(("z", "yh"), None, out), P(("z", "yh"), None, out))
    return jax.shard_map(local, mesh=split, in_specs=in_specs, out_specs=out_specs, check_vma=False)
```

```python
import math

import jax
import jax.numpy as jnp
from jax import lax
from jax.experimental import pallas as pl
from jax.experimental.pallas import tpu as pltpu
from jax.sharding import Mesh
from jax.sharding import PartitionSpec as P

DAMPING = 0.1
COLUMNS = 64
F32 = jnp.float32
BF16 = jnp.bfloat16


def split2(value):
    high = value.astype(BF16)
    low = (value - high.astype(F32)).astype(BF16)
    return high, low


def split3(value):
    high = value.astype(BF16)
    rest = value - high.astype(F32)
    middle = rest.astype(BF16)
    low = (rest - middle.astype(F32)).astype(BF16)
    return high, middle, low


def chain_kernel(where, *refs):
    pieces = refs[:8]
    out, side, turned, now, later, f1, f2, f3, u1, u2, sems = refs[8:]
    block, tokens = turned.shape
    half = COLUMNS // 2
    copies = []
    for source, row, col in placed(pieces, where[3] == 0):
        row, col = pl.multiple_of(row, 512), pl.multiple_of(col, 128)
        to = side.at[pl.ds(row, 512), pl.ds(col, 128)]
        copies.append((pltpu.make_async_copy(source, to, sems.at[len(copies)]), row, col))
        copies[-1][0].start()
    now[...] = jnp.zeros_like(now)
    later[...] = jnp.zeros_like(later)
    for copy, row, col in copies:
        copy.wait()
        turned[pl.ds(col, 128), pl.ds(row, 512)] = side[pl.ds(row, 512), pl.ds(col, 128)].T

    probe_at = pl.ds(2 * COLUMNS, 16)
    probe_row = lax.broadcasted_iota(jnp.int32, (16, block), 0)

    def times(rows, matrix):
        product = jnp.dot(rows[...], matrix[...], preferred_element_type=F32)
        probe = jnp.sum(product[2 * COLUMNS :], axis=0, keepdims=True)
        return product[:COLUMNS] + product[COLUMNS : 2 * COLUMNS], probe

    def keep(target, rows, probe=None):
        target[:COLUMNS], target[COLUMNS : 2 * COLUMNS] = split2(rows)
        if probe is not None:
            high, middle, low = (part.astype(F32) for part in split3(probe))
            stacked = jnp.where(probe_row == 0, high, jnp.where(probe_row == 1, middle, low))
            target[probe_at] = jnp.where(probe_row < 3, stacked, 0.0).astype(BF16)

    def unit():
        row = lax.broadcasted_iota(jnp.int32, (COLUMNS, block), 0)
        wanted = jnp.where(row < half, where[0] + row, where[1] + row - half)
        col = lax.broadcasted_iota(jnp.int32, (COLUMNS, block), 1)
        return jnp.where(col == wanted, 1.0, 0.0)

    later[:half] = turned[pl.ds(pl.multiple_of(where[0], half), half), :]
    later[half:COLUMNS] = turned[pl.ds(pl.multiple_of(where[1], half), half), :]
    rows, _ = times(later, side)
    rows = rows / tokens + DAMPING * unit()
    f1[...] = rows
    keep(now, rows, jnp.ones((1, block), F32))
    keep(later, *times(now, turned))
    rows, probe = times(later, side)
    rows, probe = rows / tokens + DAMPING * f1[...], probe / tokens + DAMPING
    f2[...], u1[...] = rows, probe
    keep(now, rows, probe)
    keep(later, *times(now, turned))
    rows, probe = times(later, side)
    rows, probe = rows / tokens + DAMPING * f2[...], probe / tokens + DAMPING * u1[...]
    f3[...], u2[...] = rows, probe
    keep(now, rows, probe)
    rows, probe = times(now, turned)
    keep(later, rows)
    norm = jnp.sum(u2[...] * u2[...], axis=1, keepdims=True)
    scale = (jnp.sum(probe * probe, axis=1, keepdims=True) / tokens + DAMPING * norm) / norm
    inverse = 1.0 / scale
    inverse2 = inverse * inverse
    rows, _ = times(later, side)
    a3 = f3[...] * (inverse2 * inverse)
    a4 = (rows / tokens) * (inverse2 * inverse2) + DAMPING * (a3 * inverse)
    total = 36.0 * unit() - 39.0 * (f1[...] * inverse) + 27.0 * (f2[...] * inverse2)
    keep(now, (total - 9.0 * a3 + a4) * (1.0 / (16.0 * jnp.sqrt(scale))))
    rows, _ = times(now, turned)
    for at in range(16):
        z = (where[4 + at // 4 % 2] - 2 * (at % 4)) % 8
        to = pl.ds(pl.multiple_of(((at // 8) ^ where[2]) * 1024 + z * 128, 128), 128)
        out[:, to] = rows[:, at * 128 : at * 128 + 128].astype(BF16)


def placed(pieces, first_core):
    for core in range(2):
        for outer in range(4):
            for inner in range(4):
                for other in range(2):
                    part = pieces[core * 4 + outer].at[pl.ds((inner * 2 + other) * 512, 512)]

                    def spot(x, y):
                        return y // 2 * 1024 + core * 512, (y % 2 * 8 + x * 2) * 128

                    x_first, y_first = spot(inner, outer), spot(outer, inner)
                    if core:
                        x_first, y_first = y_first, x_first
                    row, col = (jnp.where(first_core, p, q) for p, q in zip(x_first, y_first))
                    yield part, row, col + (core ^ other) * 128


def whitened_columns(pieces, where, block, tokens):
    rows = 2 * COLUMNS + 16
    passes = 8 * 2 * rows * block * tokens
    return pl.pallas_call(
        chain_kernel,
        name="whiten",
        out_shape=jax.ShapeDtypeStruct((COLUMNS, tokens), BF16),
        in_specs=[pl.BlockSpec(memory_space=pltpu.SMEM)] + [pl.BlockSpec(memory_space=pl.ANY)] * 8,
        out_specs=pl.BlockSpec(memory_space=pltpu.VMEM),
        scratch_shapes=[
            pltpu.VMEM((tokens, block), BF16),
            pltpu.VMEM((block, tokens), BF16),
            pltpu.VMEM((rows, block), BF16),
            pltpu.VMEM((rows, tokens), BF16),
            *[pltpu.VMEM((COLUMNS, block), F32)] * 3,
            *[pltpu.VMEM((1, block), F32)] * 2,
            pltpu.SemaphoreType.DMA((64,)),
        ],
        compiler_params=pltpu.CompilerParams(vmem_limit_bytes=32 * 2**20),
        cost_estimate=pl.CostEstimate(flops=passes, bytes_accessed=2 * block * tokens, transcendentals=0),
    )(where, *pieces)


def xor_swap(array, axis, mask):
    return lax.ppermute(array, axis, [(i, i ^ mask) for i in range(lax.axis_size(axis))])


def y_swap(array, mask):
    pairs = [(y % 2 * 2 + y // 2, (y ^ mask) % 2 * 2 + (y ^ mask) // 2) for y in range(4)]
    return lax.ppermute(array, ("yl", "yh"), pairs)


def plane_swap(array, first_mask, second_mask):
    def at(x, y, c):
        return (((y % 2) * 4 + x) * 2 + c) * 2 + y // 2

    pairs = []
    for x in range(4):
        for y in range(4):
            pairs.append((at(x, y, 0), at(x ^ first_mask, y ^ second_mask, 0)))
            pairs.append((at(x, y, 1), at(x ^ second_mask, y ^ first_mask, 1)))
    return lax.ppermute(array, ("yl", "x", "c", "yh"), pairs)


def twin(z):
    return (z + 1 if z % 2 else z - 1) % 8


def shared_part(activations, out_grads, z, c):
    turn = (z + 1) // 2 % 4
    pieces = (activations[:, 0], out_grads[:, 0], activations[:, 1], out_grads[:, 1])
    odd, far = turn % 2 == 1, turn >= 2
    pieces = [jnp.where(odd, pieces[(j + 1) % 4], pieces[j]) for j in range(4)]
    pieces = [jnp.where(far, pieces[(j + 2) % 4], pieces[j]) for j in range(4)]
    got = [pieces[0]]
    for shift in (1, 2, 3):
        got.append(lax.ppermute(pieces[shift], "z", [(i, (i + 2 * shift) % 8) for i in range(8)]))
    got = jnp.concatenate(got)
    across, beside = [], []
    for i in range(8):
        for j in range(2):
            if i % 2 == j:
                across.append((i * 2 + j, twin(i) * 2 + j))
            else:
                across.append((i * 2 + j, i * 2 + 1 - j))
                beside.append((i * 2 + j, twin(i) * 2 + 1 - j))
    one = lax.ppermute(got, ("z", "c"), across)
    two = lax.ppermute(got, ("z", "c"), beside)
    stays = z % 2 == c
    return jnp.concatenate([jnp.where(stays, got, one), jnp.where(stays, one, two)])


def side_pieces(part):
    masks = (1, 3, 2)
    step = {0: part, **{m: plane_swap(part, m, 0) for m in masks}}
    row = jnp.concatenate([step[m] for m in range(4)])
    wide = {0: row, **{m: plane_swap(row, 0, m) for m in masks}}
    return [wide[m] for m in range(4)]


def tile_kernel(where, acts, own, other, out, grads):
    tokens = grads.shape[1]
    for core, part in enumerate((own, other)):
        for at in range(4):
            row = pl.multiple_of(((at * 2 + core) ^ where[0]) * 32, 32)
            grads[pl.ds(row, 32), :] = part[at * 32 : at * 32 + 32, :]
    product = lax.dot_general(acts[...], grads[...], (((1,), (1,)), ((), ())), preferred_element_type=F32)
    product = (product / math.sqrt(tokens)).astype(BF16)
    for at in range(4):
        row = pl.multiple_of((at ^ where[1]) * 64, 64)
        for core in range(2):
            out[core ^ where[2], pl.ds(row, 64), :] = product[at * 64 : at * 64 + 64, core * 128 : core * 128 + 128]


def update_tile(where, acts, own, other):
    tokens = own.shape[1]
    return pl.pallas_call(
        tile_kernel,
        name="update_tile",
        out_shape=jax.ShapeDtypeStruct((2, 256, 128), BF16),
        in_specs=[pl.BlockSpec(memory_space=pltpu.SMEM)] + [pl.BlockSpec(memory_space=pltpu.VMEM)] * 3,
        out_specs=pl.BlockSpec(memory_space=pltpu.VMEM),
        scratch_shapes=[pltpu.VMEM((256, tokens), BF16)],
        compiler_params=pltpu.CompilerParams(vmem_limit_bytes=16 * 2**20),
        cost_estimate=pl.CostEstimate(flops=2 * 256 * 256 * tokens, bytes_accessed=2**21, transcendentals=0),
    )(where, acts, own, other)


def owners(step):
    pairs = []
    for z in range(8):
        act_side, grad_side = (0, 1, 1, 0)[z // 2], z // 4
        for yl in range(2):
            for c in range(2):
                to = ((act_side * 4 + yl * 2 + c) * 2 + z % 2) * 2 + (step ^ grad_side)
                pairs.append(((z * 2 + yl) * 2 + c, to))
    return pairs


def local(activations, out_grads, weight):
    tok_dev, blocks, width = activations.shape
    outs = lax.axis_size(("yl", "x", "c"))
    block = width * outs
    z, yl, x, c, yh = (lax.axis_index(a) for a in ("z", "yl", "x", "c", "yh"))
    token_count = tok_dev * lax.axis_size("z") * lax.axis_size("yh")

    pieces = side_pieces(shared_part(activations, out_grads, z, c))
    grads_whole = lax.all_gather(out_grads, ("yl", "x", "c"), axis=2, tiled=True)
    input_grad = jnp.einsum(
        "tjq,bcjq->tbc",
        grads_whole,
        weight.reshape(blocks, width, blocks, block),
        preferred_element_type=F32,
    ).astype(BF16)
    pieces, input_grad = lax.optimization_barrier((pieces, input_grad))
    pieces = pieces + [xor_swap(piece, "c", 1) for piece in pieces]

    y = yh * 2 + yl
    is_act = (z + 1) // 2 % 2 == 0
    act_first = ((yl * 2 + c) * 2 + yh) * 256 + x * 64
    grad_first = (z % 2 * 4 + x) * 256 + (y * 2 + c) * 32
    grad_second = ((1 - z % 2) * 4 + x) * 256 + (y * 2 + c) * 32

    def relative(column):
        place = column // width
        return (((place // 8) ^ yl) * 8 + ((place // 2 % 4) ^ x) * 2 + ((place % 2) ^ c)) * width + column % width

    first = relative(jnp.where(is_act, act_first, grad_first))
    second = relative(jnp.where(is_act, act_first + 32, grad_second))
    pair = jnp.where(z % 2 == 1, z + 1, z - 1) % 8
    done = whitened_columns(
        pieces,
        jnp.stack([first, second, yh, c, jnp.where(z % 2 == c, z, pair), jnp.where(z % 2 == c, pair, z)]),
        block,
        token_count,
    )

    swapped = xor_swap(done, "z", 1)
    grads = jnp.where(is_act, swapped[32:], done[:32])
    acts = jnp.where(is_act, done, swapped)
    grads = {0: grads, **{m: y_swap(grads, m) for m in (1, 3, 2)}}
    acts = {0: acts, **{m: xor_swap(acts, "x", m) for m in (1, 3, 2)}}
    grads = jnp.concatenate([grads[m] for m in range(4)])
    acts = jnp.concatenate([acts[m] for m in range(4)])
    numbers = jnp.stack([y * 2 + c, x, z // 4]).astype(jnp.int32)
    tile = update_tile(numbers, acts, grads, xor_swap(grads, "c", 1))
    tile = [lax.ppermute(tile[step], ("z", "yl", "c"), owners(step)) for step in range(2)]
    update = jnp.stack([jnp.where(c == 0, tile[0], tile[1]), jnp.where(c == 0, tile[1], tile[0])], axis=1)
    return update, input_grad


def solution(mesh):
    split = Mesh(
        mesh.devices.reshape(mesh.shape["tok"], 2, 4, 2, mesh.shape["grp"]),
        ("z", "yl", "x", "c", "yh"),
    )
    out = ("yl", "x", "c")
    in_specs = (P(("z", "yh"), None, out), P(("z", "yh"), None, out), P(None, out, None))
    out_specs = (P(("z", "yh"), None, out), P(("z", "yh"), None, out))
    return jax.shard_map(local, mesh=split, in_specs=in_specs, out_specs=out_specs, check_vma=False)
```

```python
import math

import jax
import jax.numpy as jnp
from jax import lax
from jax.experimental import pallas as pl
from jax.experimental.pallas import tpu as pltpu
from jax.sharding import Mesh
from jax.sharding import PartitionSpec as P

DAMPING = 0.1
COLUMNS = 64
F32 = jnp.float32
BF16 = jnp.bfloat16


def split2(value):
    high = value.astype(BF16)
    low = (value - high.astype(F32)).astype(BF16)
    return high, low


def split3(value):
    high = value.astype(BF16)
    rest = value - high.astype(F32)
    middle = rest.astype(BF16)
    low = (rest - middle.astype(F32)).astype(BF16)
    return high, middle, low


def chain_kernel(where, *refs):
    pieces = refs[:10]
    out, side, turned, now, later, f1, f2, f3, u1, u2, sems = refs[10:]
    block, tokens = turned.shape
    half = COLUMNS // 2
    copies = []
    for source, row, col in placed(pieces, where[3] == 0):
        row, col = pl.multiple_of(row, 512), pl.multiple_of(col, 128)
        to = side.at[pl.ds(row, 512), pl.ds(col, 128)]
        copies.append((pltpu.make_async_copy(source, to, sems.at[len(copies)]), row, col))
        copies[-1][0].start()
    now[...] = jnp.zeros_like(now)
    later[...] = jnp.zeros_like(later)
    for copy, row, col in copies:
        copy.wait()
        turned[pl.ds(col, 128), pl.ds(row, 512)] = side[pl.ds(row, 512), pl.ds(col, 128)].T

    probe_at = pl.ds(2 * COLUMNS, 16)
    probe_row = lax.broadcasted_iota(jnp.int32, (16, block), 0)

    def times(rows, matrix):
        product = jnp.dot(rows[...], matrix[...], preferred_element_type=F32)
        probe = jnp.sum(product[2 * COLUMNS :], axis=0, keepdims=True)
        return product[:COLUMNS] + product[COLUMNS : 2 * COLUMNS], probe

    def keep(target, rows, probe=None):
        target[:COLUMNS], target[COLUMNS : 2 * COLUMNS] = split2(rows)
        if probe is not None:
            high, middle, low = (part.astype(F32) for part in split3(probe))
            stacked = jnp.where(probe_row == 0, high, jnp.where(probe_row == 1, middle, low))
            target[probe_at] = jnp.where(probe_row < 3, stacked, 0.0).astype(BF16)

    def unit():
        row = lax.broadcasted_iota(jnp.int32, (COLUMNS, block), 0)
        wanted = jnp.where(row < half, where[0] + row, where[1] + row - half)
        col = lax.broadcasted_iota(jnp.int32, (COLUMNS, block), 1)
        return jnp.where(col == wanted, 1.0, 0.0)

    later[:half] = turned[pl.ds(pl.multiple_of(where[0], half), half), :]
    later[half:COLUMNS] = turned[pl.ds(pl.multiple_of(where[1], half), half), :]
    rows, _ = times(later, side)
    rows = rows / tokens + DAMPING * unit()
    f1[...] = rows
    keep(now, rows, jnp.ones((1, block), F32))
    keep(later, *times(now, turned))
    rows, probe = times(later, side)
    rows, probe = rows / tokens + DAMPING * f1[...], probe / tokens + DAMPING
    f2[...], u1[...] = rows, probe
    keep(now, rows, probe)
    keep(later, *times(now, turned))
    rows, probe = times(later, side)
    rows, probe = rows / tokens + DAMPING * f2[...], probe / tokens + DAMPING * u1[...]
    f3[...], u2[...] = rows, probe
    keep(now, rows, probe)
    rows, probe = times(now, turned)
    keep(later, rows)
    norm = jnp.sum(u2[...] * u2[...], axis=1, keepdims=True)
    scale = (jnp.sum(probe * probe, axis=1, keepdims=True) / tokens + DAMPING * norm) / norm
    inverse = 1.0 / scale
    inverse2 = inverse * inverse
    rows, _ = times(later, side)
    a3 = f3[...] * (inverse2 * inverse)
    a4 = (rows / tokens) * (inverse2 * inverse2) + DAMPING * (a3 * inverse)
    total = 36.0 * unit() - 39.0 * (f1[...] * inverse) + 27.0 * (f2[...] * inverse2)
    keep(now, (total - 9.0 * a3 + a4) * (1.0 / (16.0 * jnp.sqrt(scale))))
    rows, _ = times(now, turned)
    for at in range(16):
        z = (where[4 + at // 4 % 2] - 2 * (at % 4)) % 8
        to = pl.ds(pl.multiple_of(((at // 8) ^ where[2]) * 1024 + z * 128, 128), 128)
        out[:, to] = rows[:, at * 128 : at * 128 + 128].astype(BF16)


def placed(pieces, first_core):
    for core in range(2):
        for outer in range(4):
            for inner in range(4):
                for other in range(2):
                    piece = core * 5 + outer + (outer == 3 or outer == 2 and inner >= 2)
                    part = pieces[piece].at[pl.ds(((inner % 2 if outer == 2 else inner) * 2 + other) * 512, 512)]

                    def spot(x, y):
                        return y // 2 * 1024 + core * 512, (y % 2 * 8 + x * 2) * 128

                    x_first, y_first = spot(inner, outer), spot(outer, inner)
                    if core:
                        x_first, y_first = y_first, x_first
                    row, col = (jnp.where(first_core, p, q) for p, q in zip(x_first, y_first))
                    yield part, row, col + (core ^ other) * 128


def whitened_columns(pieces, where, block, tokens):
    rows = 2 * COLUMNS + 16
    passes = 8 * 2 * rows * block * tokens
    return pl.pallas_call(
        chain_kernel,
        name="whiten",
        out_shape=jax.ShapeDtypeStruct((COLUMNS, tokens), BF16),
        in_specs=[pl.BlockSpec(memory_space=pltpu.SMEM)] + [pl.BlockSpec(memory_space=pl.ANY)] * 10,
        out_specs=pl.BlockSpec(memory_space=pltpu.VMEM),
        scratch_shapes=[
            pltpu.VMEM((tokens, block), BF16),
            pltpu.VMEM((block, tokens), BF16),
            pltpu.VMEM((rows, block), BF16),
            pltpu.VMEM((rows, tokens), BF16),
            *[pltpu.VMEM((COLUMNS, block), F32)] * 3,
            *[pltpu.VMEM((1, block), F32)] * 2,
            pltpu.SemaphoreType.DMA((64,)),
        ],
        compiler_params=pltpu.CompilerParams(vmem_limit_bytes=32 * 2**20),
        cost_estimate=pl.CostEstimate(flops=passes, bytes_accessed=2 * block * tokens, transcendentals=0),
    )(where, *pieces)


def xor_swap(array, axis, mask):
    return lax.ppermute(array, axis, [(i, i ^ mask) for i in range(lax.axis_size(axis))])


def y_swap(array, mask):
    pairs = [(y % 2 * 2 + y // 2, (y ^ mask) % 2 * 2 + (y ^ mask) // 2) for y in range(4)]
    return lax.ppermute(array, ("yl", "yh"), pairs)


def plane_swap(array, first_mask, second_mask):
    def at(x, y, c):
        return (((y % 2) * 4 + x) * 2 + c) * 2 + y // 2

    pairs = []
    for x in range(4):
        for y in range(4):
            pairs.append((at(x, y, 0), at(x ^ first_mask, y ^ second_mask, 0)))
            pairs.append((at(x, y, 1), at(x ^ second_mask, y ^ first_mask, 1)))
    return lax.ppermute(array, ("yl", "x", "c", "yh"), pairs)


def twin(z):
    return (z + 1 if z % 2 else z - 1) % 8


def shared_part(activations, out_grads, z, c):
    turn = (z + 1) // 2 % 4
    pieces = (activations[:, 0], out_grads[:, 0], activations[:, 1], out_grads[:, 1])
    odd, far = turn % 2 == 1, turn >= 2
    pieces = [jnp.where(odd, pieces[(j + 1) % 4], pieces[j]) for j in range(4)]
    pieces = [jnp.where(far, pieces[(j + 2) % 4], pieces[j]) for j in range(4)]
    got = [pieces[0]]
    for shift in (1, 2, 3):
        got.append(lax.ppermute(pieces[shift], "z", [(i, (i + 2 * shift) % 8) for i in range(8)]))
    got = jnp.concatenate(got)
    across, beside = [], []
    for i in range(8):
        for j in range(2):
            if i % 2 == j:
                across.append((i * 2 + j, twin(i) * 2 + j))
            else:
                across.append((i * 2 + j, i * 2 + 1 - j))
                beside.append((i * 2 + j, twin(i) * 2 + 1 - j))
    one = lax.ppermute(got, ("z", "c"), across)
    two = lax.ppermute(got, ("z", "c"), beside)
    stays = z % 2 == c
    return jnp.concatenate([jnp.where(stays, got, one), jnp.where(stays, one, two)])


def side_pieces(part):
    masks = (1, 3, 2)
    step = {0: part, **{m: plane_swap(part, m, 0) for m in masks}}
    row = jnp.concatenate([step[m] for m in range(4)])
    one, three = plane_swap(row, 0, 1), plane_swap(row, 0, 3)
    two = [plane_swap(one[:2048], 0, 3), plane_swap(three[2048:], 0, 1)]
    return [row, one, *two, three]


def tile_kernel(where, acts, own, other, out, grads):
    tokens = grads.shape[1]
    for core, part in enumerate((own, other)):
        for at in range(4):
            row = pl.multiple_of(((at * 2 + core) ^ where[0]) * 32, 32)
            grads[pl.ds(row, 32), :] = part[at * 32 : at * 32 + 32, :]
    product = lax.dot_general(acts[...], grads[...], (((1,), (1,)), ((), ())), preferred_element_type=F32)
    product = (product / math.sqrt(tokens)).astype(BF16)
    for at in range(4):
        row = pl.multiple_of((at ^ where[1]) * 64, 64)
        for core in range(2):
            out[core ^ where[2], pl.ds(row, 64), :] = product[at * 64 : at * 64 + 64, core * 128 : core * 128 + 128]


def update_tile(where, acts, own, other):
    tokens = own.shape[1]
    return pl.pallas_call(
        tile_kernel,
        name="update_tile",
        out_shape=jax.ShapeDtypeStruct((2, 256, 128), BF16),
        in_specs=[pl.BlockSpec(memory_space=pltpu.SMEM)] + [pl.BlockSpec(memory_space=pltpu.VMEM)] * 3,
        out_specs=pl.BlockSpec(memory_space=pltpu.VMEM),
        scratch_shapes=[pltpu.VMEM((256, tokens), BF16)],
        compiler_params=pltpu.CompilerParams(vmem_limit_bytes=16 * 2**20),
        cost_estimate=pl.CostEstimate(flops=2 * 256 * 256 * tokens, bytes_accessed=2**21, transcendentals=0),
    )(where, acts, own, other)


def input_kernel(where, *refs):
    parts, weight, out, grads = refs[:4], refs[4], refs[5], refs[6]
    for x in range(4):
        for yl in range(2):
            for core in range(2):
                spot = (yl ^ where[0]) * 1024 + (x ^ where[1]) * 256 + (core ^ where[2]) * 128
                for side in range(2):
                    row = ((yl * 2 + core) * 2 + side) * 128
                    col = pl.multiple_of(side * 2048 + spot, 128)
                    grads[:, pl.ds(col, 128)] = parts[x][row : row + 128, :]
    product = lax.dot_general(grads[...], weight[...], (((1,), (1,)), ((), ())), preferred_element_type=F32)
    for side in range(2):
        out[side] = product[:, side * 128 : side * 128 + 128].astype(BF16)


def grads_by_weight(where, parts, weight):
    blocks, width, features = weight.shape
    tokens = parts[0].shape[0] // 8
    return pl.pallas_call(
        input_kernel,
        name="input_grad",
        out_shape=jax.ShapeDtypeStruct((blocks, tokens, width), BF16),
        in_specs=[pl.BlockSpec(memory_space=pltpu.SMEM)] + [pl.BlockSpec(memory_space=pltpu.VMEM)] * 5,
        out_specs=pl.BlockSpec(memory_space=pltpu.VMEM),
        scratch_shapes=[pltpu.VMEM((tokens, features), BF16)],
        compiler_params=pltpu.CompilerParams(vmem_limit_bytes=16 * 2**20),
        cost_estimate=pl.CostEstimate(
            flops=2 * tokens * features * blocks * width, bytes_accessed=3 * 2**20, transcendentals=0
        ),
    )(where, *parts, weight.reshape(blocks * width, features))


def owners(step):
    pairs = []
    for z in range(8):
        act_side, grad_side = (0, 1, 1, 0)[z // 2], z // 4
        for yl in range(2):
            for c in range(2):
                to = ((act_side * 4 + yl * 2 + c) * 2 + z % 2) * 2 + (step ^ grad_side)
                pairs.append(((z * 2 + yl) * 2 + c, to))
    return pairs


def local(activations, out_grads, weight):
    tok_dev, blocks, width = activations.shape
    outs = lax.axis_size(("yl", "x", "c"))
    block = width * outs
    z, yl, x, c, yh = (lax.axis_index(a) for a in ("z", "yl", "x", "c", "yh"))
    token_count = tok_dev * lax.axis_size("z") * lax.axis_size("yh")

    pieces = side_pieces(shared_part(activations, out_grads, z, c))
    pieces += [xor_swap(piece, "c", 1) for piece in pieces]
    near = jnp.concatenate([out_grads[:, 0], out_grads[:, 1]])
    near = jnp.concatenate([near, xor_swap(near, "c", 1)])
    near = jnp.concatenate([near, xor_swap(near, "yl", 1)])
    near, pieces = lax.optimization_barrier((near, pieces))
    over_x = [near] + [xor_swap(near, "x", m) for m in (1, 2, 3)]

    y = yh * 2 + yl
    is_act = (z + 1) // 2 % 2 == 0
    act_first = ((yl * 2 + c) * 2 + yh) * 256 + x * 64
    grad_first = (z % 2 * 4 + x) * 256 + (y * 2 + c) * 32
    grad_second = ((1 - z % 2) * 4 + x) * 256 + (y * 2 + c) * 32

    def relative(column):
        place = column // width
        return (((place // 8) ^ yl) * 8 + ((place // 2 % 4) ^ x) * 2 + ((place % 2) ^ c)) * width + column % width

    first = relative(jnp.where(is_act, act_first, grad_first))
    second = relative(jnp.where(is_act, act_first + 32, grad_second))
    pair = jnp.where(z % 2 == 1, z + 1, z - 1) % 8
    done = whitened_columns(
        pieces,
        jnp.stack([first, second, yh, c, jnp.where(z % 2 == c, z, pair), jnp.where(z % 2 == c, pair, z)]),
        block,
        token_count,
    )

    done, over_x = lax.optimization_barrier((done, over_x))
    input_grad = grads_by_weight(jnp.stack([yl, x, c]).astype(jnp.int32), over_x, weight)

    swapped = xor_swap(done, "z", 1)
    grads = jnp.where(is_act, swapped[32:], done[:32])
    acts = jnp.where(is_act, done, swapped)
    grads = {0: grads, **{m: y_swap(grads, m) for m in (1, 3, 2)}}
    acts = {0: acts, **{m: xor_swap(acts, "x", m) for m in (1, 3, 2)}}
    grads = jnp.concatenate([grads[m] for m in range(4)])
    acts = jnp.concatenate([acts[m] for m in range(4)])
    grads, acts, input_grad = lax.optimization_barrier((grads, acts, input_grad))
    numbers = jnp.stack([y * 2 + c, x, z // 4]).astype(jnp.int32)
    tile = update_tile(numbers, acts, grads, xor_swap(grads, "c", 1))
    tile = [lax.ppermute(tile[step], ("z", "yl", "c"), owners(step)) for step in range(2)]
    update = jnp.stack([jnp.where(c == 0, tile[0], tile[1]), jnp.where(c == 0, tile[1], tile[0])], axis=1)
    return update, input_grad.transpose(1, 0, 2)


def solution(mesh):
    split = Mesh(
        mesh.devices.reshape(mesh.shape["tok"], 2, 4, 2, mesh.shape["grp"]),
        ("z", "yl", "x", "c", "yh"),
    )
    out = ("yl", "x", "c")
    in_specs = (P(("z", "yh"), None, out), P(("z", "yh"), None, out), P(None, out, None))
    out_specs = (P(("z", "yh"), None, out), P(("z", "yh"), None, out))
    return jax.shard_map(local, mesh=split, in_specs=in_specs, out_specs=out_specs, check_vma=False)
```

```python
import math

import jax
import jax.numpy as jnp
from jax import lax
from jax.experimental import pallas as pl
from jax.experimental.pallas import tpu as pltpu
from jax.sharding import Mesh
from jax.sharding import PartitionSpec as P

DAMPING = 0.1
COLUMNS = 64
F32 = jnp.float32
BF16 = jnp.bfloat16


def split2(value):
    high = value.astype(BF16)
    low = (value - high.astype(F32)).astype(BF16)
    return high, low


def split3(value):
    high = value.astype(BF16)
    rest = value - high.astype(F32)
    middle = rest.astype(BF16)
    low = (rest - middle.astype(F32)).astype(BF16)
    return high, middle, low


def chain_kernel(where, *refs):
    pieces = refs[:16]
    out, side, turned, now, later, f1, f2, f3, u1, u2, sems = refs[16:]
    block, tokens = turned.shape
    half = COLUMNS // 2
    copies = []
    for source, row, col in placed(pieces, where[3] == 0):
        row, col = pl.multiple_of(row, 512), pl.multiple_of(col, 128)
        to = side.at[pl.ds(row, 512), pl.ds(col, 128)]
        copies.append((pltpu.make_async_copy(source, to, sems.at[len(copies)]), row, col))
        copies[-1][0].start()
    now[...] = jnp.zeros_like(now)
    later[...] = jnp.zeros_like(later)
    for copy, row, col in copies:
        copy.wait()
        turned[pl.ds(col, 128), pl.ds(row, 512)] = side[pl.ds(row, 512), pl.ds(col, 128)].T

    probe_at = pl.ds(2 * COLUMNS, 16)
    probe_row = lax.broadcasted_iota(jnp.int32, (16, block), 0)

    def times(rows, matrix):
        product = jnp.dot(rows[...], matrix[...], preferred_element_type=F32)
        probe = jnp.sum(product[2 * COLUMNS :], axis=0, keepdims=True)
        return product[:COLUMNS] + product[COLUMNS : 2 * COLUMNS], probe

    def keep(target, rows, probe=None):
        target[:COLUMNS], target[COLUMNS : 2 * COLUMNS] = split2(rows)
        if probe is not None:
            high, middle, low = (part.astype(F32) for part in split3(probe))
            stacked = jnp.where(probe_row == 0, high, jnp.where(probe_row == 1, middle, low))
            target[probe_at] = jnp.where(probe_row < 3, stacked, 0.0).astype(BF16)

    def unit():
        row = lax.broadcasted_iota(jnp.int32, (COLUMNS, block), 0)
        wanted = jnp.where(row < half, where[0] + row, where[1] + row - half)
        col = lax.broadcasted_iota(jnp.int32, (COLUMNS, block), 1)
        return jnp.where(col == wanted, 1.0, 0.0)

    later[:half] = turned[pl.ds(pl.multiple_of(where[0], half), half), :]
    later[half:COLUMNS] = turned[pl.ds(pl.multiple_of(where[1], half), half), :]
    rows, _ = times(later, side)
    rows = rows / tokens + DAMPING * unit()
    f1[...] = rows
    keep(now, rows, jnp.ones((1, block), F32))
    keep(later, *times(now, turned))
    rows, probe = times(later, side)
    rows, probe = rows / tokens + DAMPING * f1[...], probe / tokens + DAMPING
    f2[...], u1[...] = rows, probe
    keep(now, rows, probe)
    keep(later, *times(now, turned))
    rows, probe = times(later, side)
    rows, probe = rows / tokens + DAMPING * f2[...], probe / tokens + DAMPING * u1[...]
    f3[...], u2[...] = rows, probe
    keep(now, rows, probe)
    rows, probe = times(now, turned)
    keep(later, rows)
    norm = jnp.sum(u2[...] * u2[...], axis=1, keepdims=True)
    scale = (jnp.sum(probe * probe, axis=1, keepdims=True) / tokens + DAMPING * norm) / norm
    inverse = 1.0 / scale
    inverse2 = inverse * inverse
    rows, _ = times(later, side)
    a3 = f3[...] * (inverse2 * inverse)
    a4 = (rows / tokens) * (inverse2 * inverse2) + DAMPING * (a3 * inverse)
    total = 36.0 * unit() - 39.0 * (f1[...] * inverse) + 27.0 * (f2[...] * inverse2)
    keep(now, (total - 9.0 * a3 + a4) * (1.0 / (16.0 * jnp.sqrt(scale))))
    rows, _ = times(now, turned)
    for at in range(16):
        z = (where[4 + at // 4 % 2] - 2 * (at % 4)) % 8
        to = pl.ds(pl.multiple_of(((at // 8) ^ where[2]) * 1024 + z * 128, 128), 128)
        out[:, to] = rows[:, at * 128 : at * 128 + 128].astype(BF16)


def placed(pieces, first_core):
    for core in range(2):
        for outer in range(4):
            for inner in range(4):
                for other in range(2):
                    piece = pieces[core * 8 + outer * 2 + inner // 2]
                    part = piece.at[pl.ds((inner % 2 * 2 + other) * 512, 512)]

                    def spot(x, y):
                        return y // 2 * 1024 + core * 512, (y % 2 * 8 + x * 2) * 128

                    x_first, y_first = spot(inner, outer), spot(outer, inner)
                    if core:
                        x_first, y_first = y_first, x_first
                    row, col = (jnp.where(first_core, p, q) for p, q in zip(x_first, y_first))
                    yield part, row, col + (core ^ other) * 128


def whitened_columns(pieces, where, block, tokens):
    rows = 2 * COLUMNS + 16
    passes = 8 * 2 * rows * block * tokens
    return pl.pallas_call(
        chain_kernel,
        name="whiten",
        out_shape=jax.ShapeDtypeStruct((COLUMNS, tokens), BF16),
        in_specs=[pl.BlockSpec(memory_space=pltpu.SMEM)] + [pl.BlockSpec(memory_space=pl.ANY)] * 16,
        out_specs=pl.BlockSpec(memory_space=pltpu.VMEM),
        scratch_shapes=[
            pltpu.VMEM((tokens, block), BF16),
            pltpu.VMEM((block, tokens), BF16),
            pltpu.VMEM((rows, block), BF16),
            pltpu.VMEM((rows, tokens), BF16),
            *[pltpu.VMEM((COLUMNS, block), F32)] * 3,
            *[pltpu.VMEM((1, block), F32)] * 2,
            pltpu.SemaphoreType.DMA((64,)),
        ],
        compiler_params=pltpu.CompilerParams(vmem_limit_bytes=32 * 2**20),
        cost_estimate=pl.CostEstimate(flops=passes, bytes_accessed=2 * block * tokens, transcendentals=0),
    )(where, *pieces)


def xor_swap(array, axis, mask):
    return lax.ppermute(array, axis, [(i, i ^ mask) for i in range(lax.axis_size(axis))])


def y_swap(array, mask):
    pairs = [(y % 2 * 2 + y // 2, (y ^ mask) % 2 * 2 + (y ^ mask) // 2) for y in range(4)]
    return lax.ppermute(array, ("yl", "yh"), pairs)


def plane_swap(array, first_mask, second_mask):
    def at(x, y, c):
        return (((y % 2) * 4 + x) * 2 + c) * 2 + y // 2

    pairs = []
    for x in range(4):
        for y in range(4):
            pairs.append((at(x, y, 0), at(x ^ first_mask, y ^ second_mask, 0)))
            pairs.append((at(x, y, 1), at(x ^ second_mask, y ^ first_mask, 1)))
    return lax.ppermute(array, ("yl", "x", "c", "yh"), pairs)


def twin(z):
    return (z + 1 if z % 2 else z - 1) % 8


def shared_part(activations, out_grads, z, c):
    turn = (z + 1) // 2 % 4
    pieces = (activations[:, 0], out_grads[:, 0], activations[:, 1], out_grads[:, 1])
    odd, far = turn % 2 == 1, turn >= 2
    pieces = [jnp.where(odd, pieces[(j + 1) % 4], pieces[j]) for j in range(4)]
    pieces = [jnp.where(far, pieces[(j + 2) % 4], pieces[j]) for j in range(4)]
    got = [pieces[0]]
    for shift in (1, 2, 3):
        got.append(lax.ppermute(pieces[shift], "z", [(i, (i + 2 * shift) % 8) for i in range(8)]))
    got = jnp.concatenate(got)
    across, beside = [], []
    for i in range(8):
        for j in range(2):
            if i % 2 == j:
                across.append((i * 2 + j, twin(i) * 2 + j))
            else:
                across.append((i * 2 + j, i * 2 + 1 - j))
                beside.append((i * 2 + j, twin(i) * 2 + 1 - j))
    one = lax.ppermute(got, ("z", "c"), across)
    two = lax.ppermute(got, ("z", "c"), beside)
    stays = z % 2 == c
    return jnp.concatenate([jnp.where(stays, got, one), jnp.where(stays, one, two)])


def side_pieces(part):
    low = {0: jnp.concatenate([part, plane_swap(part, 1, 0)])}
    high = {0: jnp.concatenate([plane_swap(part, 2, 0), plane_swap(part, 3, 0)])}
    low |= {m: plane_swap(low[0], 0, m) for m in (1, 3)}
    high |= {m: plane_swap(high[0], 0, m) for m in (3, 1)}
    low[2], high[2] = plane_swap(low[1], 0, 3), plane_swap(high[3], 0, 1)
    near = lax.optimization_barrier([(low[m], high[m]) for m in (0, 1, 3)])
    pieces = [*near[0], *near[1], low[2], high[2], *near[2]]
    return pieces + [xor_swap(piece, "c", 1) for piece in pieces]


def tile_kernel(where, acts, own, other, out, grads):
    tokens = grads.shape[1]
    for core, part in enumerate((own, other)):
        for at in range(4):
            row = pl.multiple_of(((at * 2 + core) ^ where[0]) * 32, 32)
            grads[pl.ds(row, 32), :] = part[at * 32 : at * 32 + 32, :]
    product = lax.dot_general(acts[...], grads[...], (((1,), (1,)), ((), ())), preferred_element_type=F32)
    product = (product / math.sqrt(tokens)).astype(BF16)
    for at in range(4):
        row = pl.multiple_of((at ^ where[1]) * 64, 64)
        for core in range(2):
            out[core ^ where[2], pl.ds(row, 64), :] = product[at * 64 : at * 64 + 64, core * 128 : core * 128 + 128]


def update_tile(where, acts, own, other):
    tokens = own.shape[1]
    return pl.pallas_call(
        tile_kernel,
        name="update_tile",
        out_shape=jax.ShapeDtypeStruct((2, 256, 128), BF16),
        in_specs=[pl.BlockSpec(memory_space=pltpu.SMEM)] + [pl.BlockSpec(memory_space=pltpu.VMEM)] * 3,
        out_specs=pl.BlockSpec(memory_space=pltpu.VMEM),
        scratch_shapes=[pltpu.VMEM((256, tokens), BF16)],
        compiler_params=pltpu.CompilerParams(vmem_limit_bytes=16 * 2**20),
        cost_estimate=pl.CostEstimate(flops=2 * 256 * 256 * tokens, bytes_accessed=2**21, transcendentals=0),
    )(where, acts, own, other)


def input_kernel(where, *refs):
    parts, weight, out, grads = refs[:4], refs[4], refs[5], refs[6]
    for x in range(4):
        for yl in range(2):
            for core in range(2):
                spot = (yl ^ where[0]) * 1024 + (x ^ where[1]) * 256 + (core ^ where[2]) * 128
                for side in range(2):
                    row = ((yl * 2 + core) * 2 + side) * 128
                    col = pl.multiple_of(side * 2048 + spot, 128)
                    grads[:, pl.ds(col, 128)] = parts[x][row : row + 128, :]
    product = lax.dot_general(grads[...], weight[...], (((1,), (1,)), ((), ())), preferred_element_type=F32)
    for side in range(2):
        out[side] = product[:, side * 128 : side * 128 + 128].astype(BF16)


def grads_by_weight(where, parts, weight):
    blocks, width, features = weight.shape
    tokens = parts[0].shape[0] // 8
    return pl.pallas_call(
        input_kernel,
        name="input_grad",
        out_shape=jax.ShapeDtypeStruct((blocks, tokens, width), BF16),
        in_specs=[pl.BlockSpec(memory_space=pltpu.SMEM)] + [pl.BlockSpec(memory_space=pltpu.VMEM)] * 5,
        out_specs=pl.BlockSpec(memory_space=pltpu.VMEM),
        scratch_shapes=[pltpu.VMEM((tokens, features), BF16)],
        compiler_params=pltpu.CompilerParams(vmem_limit_bytes=16 * 2**20),
        cost_estimate=pl.CostEstimate(
            flops=2 * tokens * features * blocks * width, bytes_accessed=3 * 2**20, transcendentals=0
        ),
    )(where, *parts, weight.reshape(blocks * width, features))


def owners(step):
    pairs = []
    for z in range(8):
        act_side, grad_side = (0, 1, 1, 0)[z // 2], z // 4
        for yl in range(2):
            for c in range(2):
                to = ((act_side * 4 + yl * 2 + c) * 2 + z % 2) * 2 + (step ^ grad_side)
                pairs.append(((z * 2 + yl) * 2 + c, to))
    return pairs


def local(activations, out_grads, weight):
    tok_dev, blocks, width = activations.shape
    outs = lax.axis_size(("yl", "x", "c"))
    block = width * outs
    z, yl, x, c, yh = (lax.axis_index(a) for a in ("z", "yl", "x", "c", "yh"))
    token_count = tok_dev * lax.axis_size("z") * lax.axis_size("yh")

    pieces = side_pieces(shared_part(activations, out_grads, z, c))
    near = jnp.concatenate([out_grads[:, 0], out_grads[:, 1]])
    near = jnp.concatenate([near, xor_swap(near, "c", 1)])
    near = jnp.concatenate([near, xor_swap(near, "yl", 1)])
    near, pieces = lax.optimization_barrier((near, pieces))
    over_x = [near] + [xor_swap(near, "x", m) for m in (1, 2, 3)]

    y = yh * 2 + yl
    is_act = (z + 1) // 2 % 2 == 0
    act_first = ((yl * 2 + c) * 2 + yh) * 256 + x * 64
    grad_first = (z % 2 * 4 + x) * 256 + (y * 2 + c) * 32
    grad_second = ((1 - z % 2) * 4 + x) * 256 + (y * 2 + c) * 32

    def relative(column):
        place = column // width
        return (((place // 8) ^ yl) * 8 + ((place // 2 % 4) ^ x) * 2 + ((place % 2) ^ c)) * width + column % width

    first = relative(jnp.where(is_act, act_first, grad_first))
    second = relative(jnp.where(is_act, act_first + 32, grad_second))
    pair = jnp.where(z % 2 == 1, z + 1, z - 1) % 8
    done = whitened_columns(
        pieces,
        jnp.stack([first, second, yh, c, jnp.where(z % 2 == c, z, pair), jnp.where(z % 2 == c, pair, z)]),
        block,
        token_count,
    )

    done, over_x = lax.optimization_barrier((done, over_x))
    input_grad = grads_by_weight(jnp.stack([yl, x, c]).astype(jnp.int32), over_x, weight)

    swapped = xor_swap(done, "z", 1)
    grads = jnp.where(is_act, swapped[32:], done[:32])
    acts = jnp.where(is_act, done, swapped)
    grads = {0: grads, **{m: y_swap(grads, m) for m in (1, 3, 2)}}
    acts = {0: acts, **{m: xor_swap(acts, "x", m) for m in (1, 3, 2)}}
    grads = jnp.concatenate([grads[m] for m in range(4)])
    acts = jnp.concatenate([acts[m] for m in range(4)])
    grads, acts, input_grad = lax.optimization_barrier((grads, acts, input_grad))
    numbers = jnp.stack([y * 2 + c, x, z // 4]).astype(jnp.int32)
    tile = update_tile(numbers, acts, grads, xor_swap(grads, "c", 1))
    tile = [lax.ppermute(tile[step], ("z", "yl", "c"), owners(step)) for step in range(2)]
    update = jnp.stack([jnp.where(c == 0, tile[0], tile[1]), jnp.where(c == 0, tile[1], tile[0])], axis=1)
    return update, input_grad.transpose(1, 0, 2)


def solution(mesh):
    split = Mesh(
        mesh.devices.reshape(mesh.shape["tok"], 2, 4, 2, mesh.shape["grp"]),
        ("z", "yl", "x", "c", "yh"),
    )
    out = ("yl", "x", "c")
    in_specs = (P(("z", "yh"), None, out), P(("z", "yh"), None, out), P(None, out, None))
    out_specs = (P(("z", "yh"), None, out), P(("z", "yh"), None, out))
    return jax.shard_map(local, mesh=split, in_specs=in_specs, out_specs=out_specs, check_vma=False)
```

```python
import math

import jax
import jax.numpy as jnp
from jax import lax
from jax.experimental import pallas as pl
from jax.experimental.pallas import tpu as pltpu
from jax.sharding import Mesh
from jax.sharding import PartitionSpec as P

DAMPING = 0.1
COLUMNS = 64
F32 = jnp.float32
BF16 = jnp.bfloat16


def split2(value):
    high = value.astype(BF16)
    low = (value - high.astype(F32)).astype(BF16)
    return high, low


def split3(value):
    high = value.astype(BF16)
    rest = value - high.astype(F32)
    middle = rest.astype(BF16)
    low = (rest - middle.astype(F32)).astype(BF16)
    return high, middle, low


def chain_kernel(where, *refs):
    pieces = refs[:10]
    out, side, turned, now, later, powers, probes, scales, sems = refs[10:]
    block, tokens = turned.shape
    half = COLUMNS // 2
    copies = []
    for source, row, col in placed(pieces, where[3] == 0):
        row, col = pl.multiple_of(row, 512), pl.multiple_of(col, 128)
        to = side.at[pl.ds(row, 512), pl.ds(col, 128)]
        copies.append(pltpu.make_async_copy(source, to, sems.at[len(copies)]))
        copies[-1].start()
    now[...] = jnp.zeros_like(now)
    later[...] = jnp.zeros_like(later)
    row = lax.broadcasted_iota(jnp.int32, (COLUMNS, block), 0)
    wanted = jnp.where(row < half, where[0] + row, where[1] + row - half)
    powers[0] = jnp.where(lax.broadcasted_iota(jnp.int32, (COLUMNS, block), 1) == wanted, 1.0, 0.0)
    for core in range(2):
        for copy in copies[core * 32 : core * 32 + 32]:
            copy.wait()

        def turn(at, carry, core=core):
            rows = pl.ds(pl.multiple_of(at // 8 * 1024 + core * 512, 512), 512)
            cols = pl.ds(pl.multiple_of(at % 8 * 256, 256), 256)
            turned[cols, rows] = side[rows, cols].T
            return carry

        lax.fori_loop(0, 16, turn, 0)

    probe_at = pl.ds(2 * COLUMNS, 16)
    probe_row = lax.broadcasted_iota(jnp.int32, (16, block), 0)

    def times(rows, matrix):
        product = jnp.dot(rows[...], matrix[...], preferred_element_type=F32)
        probe = jnp.sum(product[2 * COLUMNS :], axis=0, keepdims=True)
        return product[:COLUMNS] + product[COLUMNS : 2 * COLUMNS], probe

    def keep(target, rows, probe):
        target[:COLUMNS], target[COLUMNS : 2 * COLUMNS] = split2(rows)
        high, middle, low = (part.astype(F32) for part in split3(probe))
        stacked = jnp.where(probe_row == 0, high, jnp.where(probe_row == 1, middle, low))
        target[probe_at] = jnp.where(probe_row < 3, stacked, 0.0).astype(BF16)

    later[:half] = turned[pl.ds(pl.multiple_of(where[0], half), half), :]
    later[half:COLUMNS] = turned[pl.ds(pl.multiple_of(where[1], half), half), :]

    def step(j, carry):
        rows, probe = times(later, side)
        rows = rows / tokens + DAMPING * powers[j]
        probe = jnp.where(j == 0, 1.0, probe / tokens + DAMPING * probes[...])

        @pl.when(j < 3)
        def _():
            powers[j + 1] = rows
            probes[...] = probe
            keep(now, rows, probe)

        @pl.when(j == 3)
        def _():
            inverse = 1.0 / scales[...]
            total = rows * (inverse * inverse) - 9.0 * (powers[3] * inverse)
            total = (total + 27.0 * powers[2]) * (inverse * inverse) - 39.0 * (powers[1] * inverse)
            total = (total + 36.0 * powers[0]) * (1.0 / (16.0 * jnp.sqrt(scales[...])))
            keep(now, total, probe)

        rows, probe = times(now, turned)
        norm = jnp.sum(probes[...] * probes[...], axis=1, keepdims=True)

        @pl.when(j < 3)
        def _():
            keep(later, rows, probe)
            scales[...] = (jnp.sum(probe * probe, axis=1, keepdims=True) / tokens + DAMPING * norm) / norm

        @pl.when(j == 3)
        def _():
            for at in range(16):
                z = (where[4 + at // 4 % 2] - 2 * (at % 4)) % 8
                to = pl.ds(pl.multiple_of(((at // 8) ^ where[2]) * 1024 + z * 128, 128), 128)
                out[:, to] = rows[:, at * 128 : at * 128 + 128].astype(BF16)

        return carry

    lax.fori_loop(0, 4, step, 0)


def placed(pieces, first_core):
    for core in range(2):
        for outer in range(4):
            for inner in range(4):
                for other in range(2):
                    piece = core * 5 + outer + (outer == 3 or outer == 2 and inner >= 2)
                    part = pieces[piece].at[pl.ds(((inner % 2 if outer == 2 else inner) * 2 + other) * 512, 512)]

                    def spot(x, y):
                        return y // 2 * 1024 + core * 512, (y % 2 * 8 + x * 2) * 128

                    x_first, y_first = spot(inner, outer), spot(outer, inner)
                    if core:
                        x_first, y_first = y_first, x_first
                    row, col = (jnp.where(first_core, p, q) for p, q in zip(x_first, y_first))
                    yield part, row, col + (core ^ other) * 128


def whitened_columns(pieces, where, block, tokens):
    rows = 2 * COLUMNS + 16
    passes = 8 * 2 * rows * block * tokens
    return pl.pallas_call(
        chain_kernel,
        name="whiten",
        out_shape=jax.ShapeDtypeStruct((COLUMNS, tokens), BF16),
        in_specs=[pl.BlockSpec(memory_space=pltpu.SMEM)] + [pl.BlockSpec(memory_space=pl.ANY)] * 10,
        out_specs=pl.BlockSpec(memory_space=pltpu.VMEM),
        scratch_shapes=[
            pltpu.VMEM((tokens, block), BF16),
            pltpu.VMEM((block, tokens), BF16),
            pltpu.VMEM((rows, block), BF16),
            pltpu.VMEM((rows, tokens), BF16),
            pltpu.VMEM((4, COLUMNS, block), F32),
            pltpu.VMEM((1, block), F32),
            pltpu.VMEM((1, 1), F32),
            pltpu.SemaphoreType.DMA((64,)),
        ],
        compiler_params=pltpu.CompilerParams(vmem_limit_bytes=32 * 2**20),
        cost_estimate=pl.CostEstimate(flops=passes, bytes_accessed=2 * block * tokens, transcendentals=0),
    )(where, *pieces)


def xor_swap(array, axis, mask):
    return lax.ppermute(array, axis, [(i, i ^ mask) for i in range(lax.axis_size(axis))])


def y_swap(array, mask):
    pairs = [(y % 2 * 2 + y // 2, (y ^ mask) % 2 * 2 + (y ^ mask) // 2) for y in range(4)]
    return lax.ppermute(array, ("yl", "yh"), pairs)


def plane_swap(array, first_mask, second_mask):
    def at(x, y, c):
        return (((y % 2) * 4 + x) * 2 + c) * 2 + y // 2

    pairs = []
    for x in range(4):
        for y in range(4):
            pairs.append((at(x, y, 0), at(x ^ first_mask, y ^ second_mask, 0)))
            pairs.append((at(x, y, 1), at(x ^ second_mask, y ^ first_mask, 1)))
    return lax.ppermute(array, ("yl", "x", "c", "yh"), pairs)


def twin(z):
    return (z + 1 if z % 2 else z - 1) % 8


def shared_part(activations, out_grads, z, c):
    turn = (z + 1) // 2 % 4
    pieces = (activations[:, 0], out_grads[:, 0], activations[:, 1], out_grads[:, 1])
    odd, far = turn % 2 == 1, turn >= 2
    pieces = [jnp.where(odd, pieces[(j + 1) % 4], pieces[j]) for j in range(4)]
    pieces = [jnp.where(far, pieces[(j + 2) % 4], pieces[j]) for j in range(4)]
    got = [pieces[0]]
    for shift in (1, 2, 3):
        got.append(lax.ppermute(pieces[shift], "z", [(i, (i + 2 * shift) % 8) for i in range(8)]))
    got = jnp.concatenate(got)
    across, beside = [], []
    for i in range(8):
        for j in range(2):
            if i % 2 == j:
                across.append((i * 2 + j, twin(i) * 2 + j))
            else:
                across.append((i * 2 + j, i * 2 + 1 - j))
                beside.append((i * 2 + j, twin(i) * 2 + 1 - j))
    one = lax.ppermute(got, ("z", "c"), across)
    two = lax.ppermute(got, ("z", "c"), beside)
    stays = z % 2 == c
    return jnp.concatenate([jnp.where(stays, got, one), jnp.where(stays, one, two)])


def side_pieces(part):
    masks = (1, 3, 2)
    step = {0: part, **{m: plane_swap(part, m, 0) for m in masks}}
    row = jnp.concatenate([step[m] for m in range(4)])
    one, three = plane_swap(row, 0, 1), plane_swap(row, 0, 3)
    two = [plane_swap(one[:2048], 0, 3), plane_swap(three[2048:], 0, 1)]
    return [row, one, *two, three]


def tile_kernel(where, acts, own, other, out, grads):
    tokens = grads.shape[1]
    for core, part in enumerate((own, other)):
        for at in range(4):
            row = pl.multiple_of(((at * 2 + core) ^ where[0]) * 32, 32)
            grads[pl.ds(row, 32), :] = part[at * 32 : at * 32 + 32, :]
    product = lax.dot_general(acts[...], grads[...], (((1,), (1,)), ((), ())), preferred_element_type=F32)
    product = (product / math.sqrt(tokens)).astype(BF16)
    for at in range(4):
        row = pl.multiple_of((at ^ where[1]) * 64, 64)
        for core in range(2):
            out[core ^ where[2], pl.ds(row, 64), :] = product[at * 64 : at * 64 + 64, core * 128 : core * 128 + 128]


def update_tile(where, acts, own, other):
    tokens = own.shape[1]
    return pl.pallas_call(
        tile_kernel,
        name="update_tile",
        out_shape=jax.ShapeDtypeStruct((2, 256, 128), BF16),
        in_specs=[pl.BlockSpec(memory_space=pltpu.SMEM)] + [pl.BlockSpec(memory_space=pltpu.VMEM)] * 3,
        out_specs=pl.BlockSpec(memory_space=pltpu.VMEM),
        scratch_shapes=[pltpu.VMEM((256, tokens), BF16)],
        compiler_params=pltpu.CompilerParams(vmem_limit_bytes=16 * 2**20),
        cost_estimate=pl.CostEstimate(flops=2 * 256 * 256 * tokens, bytes_accessed=2**21, transcendentals=0),
    )(where, acts, own, other)


def input_kernel(where, *refs):
    parts, weight, out, grads = refs[:4], refs[4], refs[5], refs[6]
    for x in range(4):
        for yl in range(2):
            for core in range(2):
                spot = (yl ^ where[0]) * 1024 + (x ^ where[1]) * 256 + (core ^ where[2]) * 128
                for side in range(2):
                    row = ((yl * 2 + core) * 2 + side) * 128
                    col = pl.multiple_of(side * 2048 + spot, 128)
                    grads[:, pl.ds(col, 128)] = parts[x][row : row + 128, :]
    product = lax.dot_general(grads[...], weight[...], (((1,), (1,)), ((), ())), preferred_element_type=F32)
    for side in range(2):
        out[side] = product[:, side * 128 : side * 128 + 128].astype(BF16)


def grads_by_weight(where, parts, weight):
    blocks, width, features = weight.shape
    tokens = parts[0].shape[0] // 8
    return pl.pallas_call(
        input_kernel,
        name="input_grad",
        out_shape=jax.ShapeDtypeStruct((blocks, tokens, width), BF16),
        in_specs=[pl.BlockSpec(memory_space=pltpu.SMEM)] + [pl.BlockSpec(memory_space=pltpu.VMEM)] * 5,
        out_specs=pl.BlockSpec(memory_space=pltpu.VMEM),
        scratch_shapes=[pltpu.VMEM((tokens, features), BF16)],
        compiler_params=pltpu.CompilerParams(vmem_limit_bytes=16 * 2**20),
        cost_estimate=pl.CostEstimate(
            flops=2 * tokens * features * blocks * width, bytes_accessed=3 * 2**20, transcendentals=0
        ),
    )(where, *parts, weight.reshape(blocks * width, features))


def owners(step):
    pairs = []
    for z in range(8):
        act_side, grad_side = (0, 1, 1, 0)[z // 2], z // 4
        for yl in range(2):
            for c in range(2):
                to = ((act_side * 4 + yl * 2 + c) * 2 + z % 2) * 2 + (step ^ grad_side)
                pairs.append(((z * 2 + yl) * 2 + c, to))
    return pairs


def local(activations, out_grads, weight):
    tok_dev, blocks, width = activations.shape
    outs = lax.axis_size(("yl", "x", "c"))
    block = width * outs
    z, yl, x, c, yh = (lax.axis_index(a) for a in ("z", "yl", "x", "c", "yh"))
    token_count = tok_dev * lax.axis_size("z") * lax.axis_size("yh")

    pieces = side_pieces(shared_part(activations, out_grads, z, c))
    pieces += [xor_swap(piece, "c", 1) for piece in pieces]
    near = jnp.concatenate([out_grads[:, 0], out_grads[:, 1]])
    near = jnp.concatenate([near, xor_swap(near, "c", 1)])
    near = jnp.concatenate([near, xor_swap(near, "yl", 1)])
    near, pieces = lax.optimization_barrier((near, pieces))
    over_x = [near] + [xor_swap(near, "x", m) for m in (1, 2, 3)]

    y = yh * 2 + yl
    is_act = (z + 1) // 2 % 2 == 0
    act_first = ((yl * 2 + c) * 2 + yh) * 256 + x * 64
    grad_first = (z % 2 * 4 + x) * 256 + (y * 2 + c) * 32
    grad_second = ((1 - z % 2) * 4 + x) * 256 + (y * 2 + c) * 32

    def relative(column):
        place = column // width
        return (((place // 8) ^ yl) * 8 + ((place // 2 % 4) ^ x) * 2 + ((place % 2) ^ c)) * width + column % width

    first = relative(jnp.where(is_act, act_first, grad_first))
    second = relative(jnp.where(is_act, act_first + 32, grad_second))
    pair = jnp.where(z % 2 == 1, z + 1, z - 1) % 8
    done = whitened_columns(
        pieces,
        jnp.stack([first, second, yh, c, jnp.where(z % 2 == c, z, pair), jnp.where(z % 2 == c, pair, z)]),
        block,
        token_count,
    )

    done, over_x = lax.optimization_barrier((done, over_x))
    input_grad = grads_by_weight(jnp.stack([yl, x, c]).astype(jnp.int32), over_x, weight)

    swapped = xor_swap(done, "z", 1)
    grads = jnp.where(is_act, swapped[32:], done[:32])
    acts = jnp.where(is_act, done, swapped)
    grads = {0: grads, **{m: y_swap(grads, m) for m in (1, 3, 2)}}
    acts = {0: acts, **{m: xor_swap(acts, "x", m) for m in (1, 3, 2)}}
    grads = jnp.concatenate([grads[m] for m in range(4)])
    acts = jnp.concatenate([acts[m] for m in range(4)])
    grads, acts, input_grad = lax.optimization_barrier((grads, acts, input_grad))
    numbers = jnp.stack([y * 2 + c, x, z // 4]).astype(jnp.int32)
    tile = update_tile(numbers, acts, grads, xor_swap(grads, "c", 1))
    tile = [lax.ppermute(tile[step], ("z", "yl", "c"), owners(step)) for step in range(2)]
    update = jnp.stack([jnp.where(c == 0, tile[0], tile[1]), jnp.where(c == 0, tile[1], tile[0])], axis=1)
    return update, input_grad.transpose(1, 0, 2)


def solution(mesh):
    split = Mesh(
        mesh.devices.reshape(mesh.shape["tok"], 2, 4, 2, mesh.shape["grp"]),
        ("z", "yl", "x", "c", "yh"),
    )
    out = ("yl", "x", "c")
    in_specs = (P(("z", "yh"), None, out), P(("z", "yh"), None, out), P(None, out, None))
    out_specs = (P(("z", "yh"), None, out), P(("z", "yh"), None, out))
    return jax.shard_map(local, mesh=split, in_specs=in_specs, out_specs=out_specs, check_vma=False)
```

```python
import math

import jax
import jax.numpy as jnp
from jax import lax
from jax.experimental import pallas as pl
from jax.experimental.pallas import tpu as pltpu
from jax.sharding import Mesh
from jax.sharding import PartitionSpec as P

DAMPING = 0.1
COLUMNS = 64
F32 = jnp.float32
BF16 = jnp.bfloat16


def split2(value):
    high = value.astype(BF16)
    low = (value - high.astype(F32)).astype(BF16)
    return high, low


def split3(value):
    high = value.astype(BF16)
    rest = value - high.astype(F32)
    middle = rest.astype(BF16)
    low = (rest - middle.astype(F32)).astype(BF16)
    return high, middle, low


def chain_kernel(where, *refs):
    pieces = refs[:10]
    out, side, turned, now, later, f1, f2, f3, u1, u2, sems = refs[10:]
    block, tokens = turned.shape
    half = COLUMNS // 2
    copies = []
    for source, row, col in placed(pieces, where[3] == 0):
        row, col = pl.multiple_of(row, 512), pl.multiple_of(col, 128)
        to = side.at[pl.ds(row, 512), pl.ds(col, 128)]
        copies.append((pltpu.make_async_copy(source, to, sems.at[len(copies)]), row, col))
        copies[-1][0].start()
    now[...] = jnp.zeros_like(now)
    later[...] = jnp.zeros_like(later)
    for copy, row, col in copies:
        copy.wait()
        turned[pl.ds(col, 128), pl.ds(row, 512)] = side[pl.ds(row, 512), pl.ds(col, 128)].T

    probe_at = pl.ds(2 * COLUMNS, 16)
    probe_row = lax.broadcasted_iota(jnp.int32, (16, block), 0)

    def times(rows, matrix):
        product = jnp.dot(rows[...], matrix[...], preferred_element_type=F32)
        probe = jnp.sum(product[2 * COLUMNS :], axis=0, keepdims=True)
        return product[:COLUMNS] + product[COLUMNS : 2 * COLUMNS], probe

    def keep(target, rows, probe=None):
        target[:COLUMNS], target[COLUMNS : 2 * COLUMNS] = split2(rows)
        if probe is not None:
            high, middle, low = (part.astype(F32) for part in split3(probe))
            stacked = jnp.where(probe_row == 0, high, jnp.where(probe_row == 1, middle, low))
            target[probe_at] = jnp.where(probe_row < 3, stacked, 0.0).astype(BF16)

    def unit():
        row = lax.broadcasted_iota(jnp.int32, (COLUMNS, block), 0)
        wanted = jnp.where(row < half, where[0] + row, where[1] + row - half)
        col = lax.broadcasted_iota(jnp.int32, (COLUMNS, block), 1)
        return jnp.where(col == wanted, 1.0, 0.0)

    later[:half] = turned[pl.ds(pl.multiple_of(where[0], half), half), :]
    later[half:COLUMNS] = turned[pl.ds(pl.multiple_of(where[1], half), half), :]
    rows, _ = times(later, side)
    rows = rows / tokens + DAMPING * unit()
    f1[...] = rows
    keep(now, rows, jnp.ones((1, block), F32))
    keep(later, *times(now, turned))
    rows, probe = times(later, side)
    rows, probe = rows / tokens + DAMPING * f1[...], probe / tokens + DAMPING
    f2[...], u1[...] = rows, probe
    keep(now, rows, probe)
    keep(later, *times(now, turned))
    rows, probe = times(later, side)
    rows, probe = rows / tokens + DAMPING * f2[...], probe / tokens + DAMPING * u1[...]
    f3[...], u2[...] = rows, probe
    keep(now, rows, probe)
    rows, probe = times(now, turned)
    keep(later, rows)
    norm = jnp.sum(u2[...] * u2[...], axis=1, keepdims=True)
    scale = (jnp.sum(probe * probe, axis=1, keepdims=True) / tokens + DAMPING * norm) / norm
    inverse = 1.0 / scale
    inverse2 = inverse * inverse
    rows, _ = times(later, side)
    a3 = f3[...] * (inverse2 * inverse)
    a4 = (rows / tokens) * (inverse2 * inverse2) + DAMPING * (a3 * inverse)
    total = 36.0 * unit() - 39.0 * (f1[...] * inverse) + 27.0 * (f2[...] * inverse2)
    keep(now, (total - 9.0 * a3 + a4) * (1.0 / (16.0 * jnp.sqrt(scale))))
    rows, _ = times(now, turned)
    for at in range(16):
        z = (where[4 + at // 4 % 2] - 2 * (at % 4)) % 8
        to = pl.ds(pl.multiple_of(((at // 8) ^ where[2]) * 1024 + z * 128, 128), 128)
        out[:, to] = rows[:, at * 128 : at * 128 + 128].astype(BF16)


def placed(pieces, first_core):
    for core in range(2):
        for outer in range(4):
            for inner in range(4):
                for other in range(2):
                    piece = core * 5 + outer + (outer == 3 or outer == 2 and inner >= 2)
                    part = pieces[piece].at[pl.ds(((inner % 2 if outer == 2 else inner) * 2 + other) * 512, 512)]

                    def spot(x, y):
                        return y // 2 * 1024 + core * 512, (y % 2 * 8 + x * 2) * 128

                    x_first, y_first = spot(inner, outer), spot(outer, inner)
                    if core:
                        x_first, y_first = y_first, x_first
                    row, col = (jnp.where(first_core, p, q) for p, q in zip(x_first, y_first))
                    yield part, row, col + (core ^ other) * 128


def whitened_columns(pieces, where, block, tokens):
    rows = 2 * COLUMNS + 16
    passes = 8 * 2 * rows * block * tokens
    return pl.pallas_call(
        chain_kernel,
        name="whiten",
        out_shape=jax.ShapeDtypeStruct((COLUMNS, tokens), BF16),
        in_specs=[pl.BlockSpec(memory_space=pltpu.SMEM)] + [pl.BlockSpec(memory_space=pl.ANY)] * 10,
        out_specs=pl.BlockSpec(memory_space=pltpu.VMEM),
        scratch_shapes=[
            pltpu.VMEM((tokens, block), BF16),
            pltpu.VMEM((block, tokens), BF16),
            pltpu.VMEM((rows, block), BF16),
            pltpu.VMEM((rows, tokens), BF16),
            *[pltpu.VMEM((COLUMNS, block), F32)] * 3,
            *[pltpu.VMEM((1, block), F32)] * 2,
            pltpu.SemaphoreType.DMA((64,)),
        ],
        compiler_params=pltpu.CompilerParams(vmem_limit_bytes=32 * 2**20),
        cost_estimate=pl.CostEstimate(flops=passes, bytes_accessed=2 * block * tokens, transcendentals=0),
    )(where, *pieces)


def xor_swap(array, axis, mask):
    return lax.ppermute(array, axis, [(i, i ^ mask) for i in range(lax.axis_size(axis))])


def y_swap(array, mask):
    pairs = [(y % 2 * 2 + y // 2, (y ^ mask) % 2 * 2 + (y ^ mask) // 2) for y in range(4)]
    return lax.ppermute(array, ("yl", "yh"), pairs)


def plane_swap(array, first_mask, second_mask):
    def at(x, y, c):
        return (((y % 2) * 4 + x) * 2 + c) * 2 + y // 2

    pairs = []
    for x in range(4):
        for y in range(4):
            pairs.append((at(x, y, 0), at(x ^ first_mask, y ^ second_mask, 0)))
            pairs.append((at(x, y, 1), at(x ^ second_mask, y ^ first_mask, 1)))
    return lax.ppermute(array, ("yl", "x", "c", "yh"), pairs)


def twin(z):
    return (z + 1 if z % 2 else z - 1) % 8


def shared_part(activations, out_grads, z, c):
    turn = (z + 1) // 2 % 4
    pieces = (activations[:, 0], out_grads[:, 0], activations[:, 1], out_grads[:, 1])
    odd, far = turn % 2 == 1, turn >= 2
    pieces = [jnp.where(odd, pieces[(j + 1) % 4], pieces[j]) for j in range(4)]
    pieces = [jnp.where(far, pieces[(j + 2) % 4], pieces[j]) for j in range(4)]
    got = [pieces[0]]
    for shift in (1, 2, 3):
        got.append(lax.ppermute(pieces[shift], "z", [(i, (i + 2 * shift) % 8) for i in range(8)]))
    got = jnp.concatenate(got)
    across, beside = [], []
    for i in range(8):
        across += [(i * 2, twin(i) * 2 + 1), (i * 2 + 1, i * 2)]
        beside.append((i * 2 + 1, twin(i) * 2 + 1))
    one = lax.ppermute(got, ("z", "c"), across)
    two = lax.ppermute(got, ("z", "c"), beside)
    return jnp.concatenate([jnp.where(c == 0, got, two), one])


def side_pieces(part):
    masks = (1, 3, 2)
    step = {0: part, **{m: plane_swap(part, m, 0) for m in masks}}
    row = jnp.concatenate([step[m] for m in range(4)])
    one, three = plane_swap(row, 0, 1), plane_swap(row, 0, 3)
    two = [plane_swap(one[:2048], 0, 3), plane_swap(three[2048:], 0, 1)]
    return [row, one, *two, three]


def tile_kernel(where, acts, own, other, out, grads):
    tokens = grads.shape[1]
    for core, part in enumerate((own, other)):
        for at in range(4):
            row = pl.multiple_of(((at * 2 + core) ^ where[0]) * 32, 32)
            grads[pl.ds(row, 32), :] = part[at * 32 : at * 32 + 32, :]
    product = lax.dot_general(acts[...], grads[...], (((1,), (1,)), ((), ())), preferred_element_type=F32)
    product = (product / math.sqrt(tokens)).astype(BF16)
    for at in range(4):
        row = pl.multiple_of((at ^ where[1]) * 64, 64)
        for core in range(2):
            out[core ^ where[2], pl.ds(row, 64), :] = product[at * 64 : at * 64 + 64, core * 128 : core * 128 + 128]


def update_tile(where, acts, own, other):
    tokens = own.shape[1]
    return pl.pallas_call(
        tile_kernel,
        name="update_tile",
        out_shape=jax.ShapeDtypeStruct((2, 256, 128), BF16),
        in_specs=[pl.BlockSpec(memory_space=pltpu.SMEM)] + [pl.BlockSpec(memory_space=pltpu.VMEM)] * 3,
        out_specs=pl.BlockSpec(memory_space=pltpu.VMEM),
        scratch_shapes=[pltpu.VMEM((256, tokens), BF16)],
        compiler_params=pltpu.CompilerParams(vmem_limit_bytes=16 * 2**20),
        cost_estimate=pl.CostEstimate(flops=2 * 256 * 256 * tokens, bytes_accessed=2**21, transcendentals=0),
    )(where, acts, own, other)


def input_kernel(where, *refs):
    parts, weight, out, grads = refs[:4], refs[4], refs[5], refs[6]
    for x in range(4):
        for yl in range(2):
            for core in range(2):
                spot = (yl ^ where[0]) * 1024 + (x ^ where[1]) * 256 + (core ^ where[2]) * 128
                for side in range(2):
                    row = ((yl * 2 + core) * 2 + side) * 128
                    col = pl.multiple_of(side * 2048 + spot, 128)
                    grads[:, pl.ds(col, 128)] = parts[x][row : row + 128, :]
    product = lax.dot_general(grads[...], weight[...], (((1,), (1,)), ((), ())), preferred_element_type=F32)
    for side in range(2):
        out[side] = product[:, side * 128 : side * 128 + 128].astype(BF16)


def grads_by_weight(where, parts, weight):
    blocks, width, features = weight.shape
    tokens = parts[0].shape[0] // 8
    return pl.pallas_call(
        input_kernel,
        name="input_grad",
        out_shape=jax.ShapeDtypeStruct((blocks, tokens, width), BF16),
        in_specs=[pl.BlockSpec(memory_space=pltpu.SMEM)] + [pl.BlockSpec(memory_space=pltpu.VMEM)] * 5,
        out_specs=pl.BlockSpec(memory_space=pltpu.VMEM),
        scratch_shapes=[pltpu.VMEM((tokens, features), BF16)],
        compiler_params=pltpu.CompilerParams(vmem_limit_bytes=16 * 2**20),
        cost_estimate=pl.CostEstimate(
            flops=2 * tokens * features * blocks * width, bytes_accessed=3 * 2**20, transcendentals=0
        ),
    )(where, *parts, weight.reshape(blocks * width, features))


def owners(step):
    pairs = []
    for z in range(8):
        act_side, grad_side = (0, 1, 1, 0)[z // 2], z // 4
        for yl in range(2):
            for c in range(2):
                to = ((act_side * 4 + yl * 2 + c) * 2 + z % 2) * 2 + (step ^ grad_side)
                pairs.append(((z * 2 + yl) * 2 + c, to))
    return pairs


def local(activations, out_grads, weight):
    tok_dev, blocks, width = activations.shape
    outs = lax.axis_size(("yl", "x", "c"))
    block = width * outs
    z, yl, x, c, yh = (lax.axis_index(a) for a in ("z", "yl", "x", "c", "yh"))
    token_count = tok_dev * lax.axis_size("z") * lax.axis_size("yh")

    pieces = side_pieces(shared_part(activations, out_grads, z, c))
    pieces += [xor_swap(piece, "c", 1) for piece in pieces]
    near = jnp.concatenate([out_grads[:, 0], out_grads[:, 1]])
    near = jnp.concatenate([near, xor_swap(near, "c", 1)])
    near = jnp.concatenate([near, xor_swap(near, "yl", 1)])
    near, pieces = lax.optimization_barrier((near, pieces))
    over_x = [near] + [xor_swap(near, "x", m) for m in (1, 2, 3)]

    y = yh * 2 + yl
    is_act = (z + 1) // 2 % 2 == 0
    act_first = ((yl * 2 + c) * 2 + yh) * 256 + x * 64
    grad_first = (z % 2 * 4 + x) * 256 + (y * 2 + c) * 32
    grad_second = ((1 - z % 2) * 4 + x) * 256 + (y * 2 + c) * 32

    def relative(column):
        place = column // width
        return (((place // 8) ^ yl) * 8 + ((place // 2 % 4) ^ x) * 2 + ((place % 2) ^ c)) * width + column % width

    first = relative(jnp.where(is_act, act_first, grad_first))
    second = relative(jnp.where(is_act, act_first + 32, grad_second))
    pair = jnp.where(z % 2 == 1, z + 1, z - 1) % 8
    done = whitened_columns(
        pieces,
        jnp.stack([first, second, yh, c, jnp.where(c == 0, z, pair), jnp.where(c == 0, pair, z)]),
        block,
        token_count,
    )

    done, over_x = lax.optimization_barrier((done, over_x))
    input_grad = grads_by_weight(jnp.stack([yl, x, c]).astype(jnp.int32), over_x, weight)

    swapped = xor_swap(done, "z", 1)
    grads = jnp.where(is_act, swapped[32:], done[:32])
    acts = jnp.where(is_act, done, swapped)
    grads = {0: grads, **{m: y_swap(grads, m) for m in (1, 3, 2)}}
    acts = {0: acts, **{m: xor_swap(acts, "x", m) for m in (1, 3, 2)}}
    grads = jnp.concatenate([grads[m] for m in range(4)])
    acts = jnp.concatenate([acts[m] for m in range(4)])
    grads, acts, input_grad = lax.optimization_barrier((grads, acts, input_grad))
    numbers = jnp.stack([y * 2 + c, x, z // 4]).astype(jnp.int32)
    tile = update_tile(numbers, acts, grads, xor_swap(grads, "c", 1))
    tile = [lax.ppermute(tile[step], ("z", "yl", "c"), owners(step)) for step in range(2)]
    update = jnp.stack([jnp.where(c == 0, tile[0], tile[1]), jnp.where(c == 0, tile[1], tile[0])], axis=1)
    return update, input_grad.transpose(1, 0, 2)


def solution(mesh):
    split = Mesh(
        mesh.devices.reshape(mesh.shape["tok"], 2, 4, 2, mesh.shape["grp"]),
        ("z", "yl", "x", "c", "yh"),
    )
    out = ("yl", "x", "c")
    in_specs = (P(("z", "yh"), None, out), P(("z", "yh"), None, out), P(None, out, None))
    out_specs = (P(("z", "yh"), None, out), P(("z", "yh"), None, out))
    return jax.shard_map(local, mesh=split, in_specs=in_specs, out_specs=out_specs, check_vma=False)
```

```python
import math

import jax
import jax.numpy as jnp
from jax import lax
from jax.experimental import pallas as pl
from jax.experimental.pallas import tpu as pltpu
from jax.sharding import Mesh
from jax.sharding import PartitionSpec as P

DAMPING = 0.1
COLUMNS = 64
F32 = jnp.float32
BF16 = jnp.bfloat16


def split2(value):
    high = value.astype(BF16)
    low = (value - high.astype(F32)).astype(BF16)
    return high, low


def split3(value):
    high = value.astype(BF16)
    rest = value - high.astype(F32)
    middle = rest.astype(BF16)
    low = (rest - middle.astype(F32)).astype(BF16)
    return high, middle, low


def chain_kernel(where, *refs):
    pieces = refs[:10]
    out, side, turned, now, later, f1, f2, f3, u1, u2, sems = refs[10:]
    block, tokens = turned.shape
    half = COLUMNS // 2
    copies = []
    for source, row, col in placed(pieces, where[3] == 0):
        row, col = pl.multiple_of(row, 512), pl.multiple_of(col, 128)
        to = side.at[pl.ds(row, 512), pl.ds(col, 128)]
        copies.append((pltpu.make_async_copy(source, to, sems.at[len(copies)]), row, col))
        copies[-1][0].start()
    now[...] = jnp.zeros_like(now)
    later[...] = jnp.zeros_like(later)
    for copy, row, col in copies:
        copy.wait()
        turned[pl.ds(col, 128), pl.ds(row, 512)] = side[pl.ds(row, 512), pl.ds(col, 128)].T

    probe_at = pl.ds(2 * COLUMNS, 16)
    probe_row = lax.broadcasted_iota(jnp.int32, (16, block), 0)

    def times(rows, matrix):
        product = jnp.dot(rows[...], matrix[...], preferred_element_type=F32)
        probe = jnp.sum(product[2 * COLUMNS :], axis=0, keepdims=True)
        return product[:COLUMNS] + product[COLUMNS : 2 * COLUMNS], probe

    def keep(target, rows, probe=None):
        target[:COLUMNS], target[COLUMNS : 2 * COLUMNS] = split2(rows)
        if probe is not None:
            high, middle, low = (part.astype(F32) for part in split3(probe))
            stacked = jnp.where(probe_row == 0, high, jnp.where(probe_row == 1, middle, low))
            target[probe_at] = jnp.where(probe_row < 3, stacked, 0.0).astype(BF16)

    def unit():
        row = lax.broadcasted_iota(jnp.int32, (COLUMNS, block), 0)
        wanted = jnp.where(row < half, where[0] + row, where[1] + row - half)
        col = lax.broadcasted_iota(jnp.int32, (COLUMNS, block), 1)
        return jnp.where(col == wanted, 1.0, 0.0)

    later[:half] = turned[pl.ds(pl.multiple_of(where[0], half), half), :]
    later[half:COLUMNS] = turned[pl.ds(pl.multiple_of(where[1], half), half), :]
    rows, _ = times(later, side)
    rows = rows / tokens + DAMPING * unit()
    f1[...] = rows
    keep(now, rows, jnp.ones((1, block), F32))
    keep(later, *times(now, turned))
    rows, probe = times(later, side)
    rows, probe = rows / tokens + DAMPING * f1[...], probe / tokens + DAMPING
    f2[...], u1[...] = rows, probe
    keep(now, rows, probe)
    keep(later, *times(now, turned))
    rows, probe = times(later, side)
    rows, probe = rows / tokens + DAMPING * f2[...], probe / tokens + DAMPING * u1[...]
    f3[...], u2[...] = rows, probe
    keep(now, rows, probe)
    rows, probe = times(now, turned)
    keep(later, rows)
    norm = jnp.sum(u2[...] * u2[...], axis=1, keepdims=True)
    scale = (jnp.sum(probe * probe, axis=1, keepdims=True) / tokens + DAMPING * norm) / norm
    inverse = 1.0 / scale
    inverse2 = inverse * inverse
    rows, _ = times(later, side)
    a3 = f3[...] * (inverse2 * inverse)
    a4 = (rows / tokens) * (inverse2 * inverse2) + DAMPING * (a3 * inverse)
    total = 36.0 * unit() - 39.0 * (f1[...] * inverse) + 27.0 * (f2[...] * inverse2)
    keep(now, (total - 9.0 * a3 + a4) * (1.0 / (16.0 * jnp.sqrt(scale))))
    rows, _ = times(now, turned)
    for at in range(16):
        z = (where[4 + at // 4 % 2] - 2 * (at % 4)) % 8
        to = pl.ds(pl.multiple_of(((at // 8) ^ where[2]) * 1024 + z * 128, 128), 128)
        out[:, to] = rows[:, at * 128 : at * 128 + 128].astype(BF16)


def placed(pieces, first_core):
    for core in range(2):
        for outer in range(4):
            for inner in range(4):
                for other in range(2):
                    piece = core * 5 + outer + (outer == 3 or outer == 2 and inner >= 2)
                    part = pieces[piece].at[pl.ds(((inner % 2 if outer == 2 else inner) * 2 + other) * 512, 512)]

                    def spot(x, y):
                        return y // 2 * 1024 + core * 512, (y % 2 * 8 + x * 2) * 128

                    x_first, y_first = spot(inner, outer), spot(outer, inner)
                    if core:
                        x_first, y_first = y_first, x_first
                    row, col = (jnp.where(first_core, p, q) for p, q in zip(x_first, y_first))
                    yield part, row, col + (core ^ other) * 128


def whitened_columns(pieces, where, block, tokens):
    rows = 2 * COLUMNS + 16
    passes = 8 * 2 * rows * block * tokens
    return pl.pallas_call(
        chain_kernel,
        name="whiten",
        out_shape=jax.ShapeDtypeStruct((COLUMNS, tokens), BF16),
        in_specs=[pl.BlockSpec(memory_space=pltpu.SMEM)] + [pl.BlockSpec(memory_space=pl.ANY)] * 10,
        out_specs=pl.BlockSpec(memory_space=pltpu.VMEM),
        scratch_shapes=[
            pltpu.VMEM((tokens, block), BF16),
            pltpu.VMEM((block, tokens), BF16),
            pltpu.VMEM((rows, block), BF16),
            pltpu.VMEM((rows, tokens), BF16),
            *[pltpu.VMEM((COLUMNS, block), F32)] * 3,
            *[pltpu.VMEM((1, block), F32)] * 2,
            pltpu.SemaphoreType.DMA((64,)),
        ],
        compiler_params=pltpu.CompilerParams(vmem_limit_bytes=32 * 2**20),
        cost_estimate=pl.CostEstimate(flops=passes, bytes_accessed=2 * block * tokens, transcendentals=0),
    )(where, *pieces)


def xor_swap(array, axis, mask):
    return lax.ppermute(array, axis, [(i, i ^ mask) for i in range(lax.axis_size(axis))])


def y_swap(array, mask):
    pairs = [(y % 2 * 2 + y // 2, (y ^ mask) % 2 * 2 + (y ^ mask) // 2) for y in range(4)]
    return lax.ppermute(array, ("yl", "yh"), pairs)


def plane_swap(array, first_mask, second_mask):
    def at(x, y, c):
        return (((y % 2) * 4 + x) * 2 + c) * 2 + y // 2

    pairs = []
    for x in range(4):
        for y in range(4):
            pairs.append((at(x, y, 0), at(x ^ first_mask, y ^ second_mask, 0)))
            pairs.append((at(x, y, 1), at(x ^ second_mask, y ^ first_mask, 1)))
    return lax.ppermute(array, ("yl", "x", "c", "yh"), pairs)


def twin(z):
    return (z + 1 if z % 2 else z - 1) % 8


def shared_part(activations, out_grads, z, c):
    turn = (z + 1) // 2 % 4
    pieces = (activations[:, 0], out_grads[:, 0], activations[:, 1], out_grads[:, 1])
    odd, far = turn % 2 == 1, turn >= 2
    pieces = [jnp.where(odd, pieces[(j + 1) % 4], pieces[j]) for j in range(4)]
    pieces = [jnp.where(far, pieces[(j + 2) % 4], pieces[j]) for j in range(4)]
    got = [pieces[0]]
    for shift in (1, 2, 3):
        got.append(lax.ppermute(pieces[shift], "z", [(i, (i + 2 * shift) % 8) for i in range(8)]))
    got = jnp.concatenate(got)
    across, beside = [], []
    for i in range(8):
        across += [(i * 2, twin(i) * 2 + 1), (i * 2 + 1, i * 2)]
        beside.append((i * 2 + 1, twin(i) * 2 + 1))
    one = lax.ppermute(got, ("z", "c"), across)
    two = lax.ppermute(got, ("z", "c"), beside)
    return jnp.concatenate([jnp.where(c == 0, got, two), one])


def side_pieces(part):
    masks = (1, 3, 2)
    step = {0: part, **{m: plane_swap(part, m, 0) for m in masks}}
    row = jnp.concatenate([step[m] for m in range(4)])
    one, three = plane_swap(row, 0, 1), plane_swap(row, 0, 3)
    two = [plane_swap(one[:2048], 0, 3), plane_swap(three[2048:], 0, 1)]
    return [row, one, *two, three]


def tile_kernel(where, acts, own, other, out, grads):
    tokens = grads.shape[1]
    for core, part in enumerate((own, other)):
        for at in range(4):
            row = pl.multiple_of(((at * 2 + core) ^ where[0]) * 32, 32)
            grads[pl.ds(row, 32), :] = part[at * 32 : at * 32 + 32, :]
    product = lax.dot_general(acts[...], grads[...], (((1,), (1,)), ((), ())), preferred_element_type=F32)
    product = (product / math.sqrt(tokens)).astype(BF16)
    for at in range(4):
        row = pl.multiple_of((at ^ where[1]) * 64, 64)
        for core in range(2):
            out[core, pl.ds(row, 64), :] = product[at * 64 : at * 64 + 64, core * 128 : core * 128 + 128]


def update_tile(where, acts, own, other):
    tokens = own.shape[1]
    return pl.pallas_call(
        tile_kernel,
        name="update_tile",
        out_shape=jax.ShapeDtypeStruct((2, 256, 128), BF16),
        in_specs=[pl.BlockSpec(memory_space=pltpu.SMEM)] + [pl.BlockSpec(memory_space=pltpu.VMEM)] * 3,
        out_specs=pl.BlockSpec(memory_space=pltpu.VMEM),
        scratch_shapes=[pltpu.VMEM((256, tokens), BF16)],
        compiler_params=pltpu.CompilerParams(vmem_limit_bytes=16 * 2**20),
        cost_estimate=pl.CostEstimate(flops=2 * 256 * 256 * tokens, bytes_accessed=2**21, transcendentals=0),
    )(where, acts, own, other)


def input_kernel(where, *refs):
    parts, weight, out, grads = refs[:4], refs[4], refs[5], refs[6]
    for x in range(4):
        for yl in range(2):
            for core in range(2):
                spot = (yl ^ where[0]) * 1024 + (x ^ where[1]) * 256 + (core ^ where[2]) * 128
                for side in range(2):
                    row = ((yl * 2 + core) * 2 + side) * 128
                    col = pl.multiple_of(side * 2048 + spot, 128)
                    grads[:, pl.ds(col, 128)] = parts[x][row : row + 128, :]
    product = lax.dot_general(grads[...], weight[...], (((1,), (1,)), ((), ())), preferred_element_type=F32)
    for side in range(2):
        out[side] = product[:, side * 128 : side * 128 + 128].astype(BF16)


def grads_by_weight(where, parts, weight):
    blocks, width, features = weight.shape
    tokens = parts[0].shape[0] // 8
    return pl.pallas_call(
        input_kernel,
        name="input_grad",
        out_shape=jax.ShapeDtypeStruct((blocks, tokens, width), BF16),
        in_specs=[pl.BlockSpec(memory_space=pltpu.SMEM)] + [pl.BlockSpec(memory_space=pltpu.VMEM)] * 5,
        out_specs=pl.BlockSpec(memory_space=pltpu.VMEM),
        scratch_shapes=[pltpu.VMEM((tokens, features), BF16)],
        compiler_params=pltpu.CompilerParams(vmem_limit_bytes=16 * 2**20),
        cost_estimate=pl.CostEstimate(
            flops=2 * tokens * features * blocks * width, bytes_accessed=3 * 2**20, transcendentals=0
        ),
    )(where, *parts, weight.reshape(blocks * width, features))


def owners():
    pairs = []
    for z in range(8):
        act_side, grad_side = (0, 1, 1, 0)[z // 2], z // 4
        for yl in range(2):
            for c in range(2):
                to = ((act_side * 4 + yl * 2 + c) * 2 + z % 2) * 2 + grad_side
                pairs.append(((z * 2 + yl) * 2 + c, to))
    return pairs


def local(activations, out_grads, weight):
    tok_dev, blocks, width = activations.shape
    outs = lax.axis_size(("yl", "x", "c"))
    block = width * outs
    z, yl, x, c, yh = (lax.axis_index(a) for a in ("z", "yl", "x", "c", "yh"))
    token_count = tok_dev * lax.axis_size("z") * lax.axis_size("yh")

    pieces = side_pieces(shared_part(activations, out_grads, z, c))
    pieces += [xor_swap(piece, "c", 1) for piece in pieces]
    near = jnp.concatenate([out_grads[:, 0], out_grads[:, 1]])
    near = jnp.concatenate([near, xor_swap(near, "c", 1)])
    near = jnp.concatenate([near, xor_swap(near, "yl", 1)])
    near, pieces = lax.optimization_barrier((near, pieces))
    over_x = [near] + [xor_swap(near, "x", m) for m in (1, 2, 3)]

    y = yh * 2 + yl
    is_act = (z + 1) // 2 % 2 == 0
    act_first = ((yl * 2 + c) * 2 + yh) * 256 + x * 64
    grad_first = (z % 2 * 4 + x) * 256 + (y * 2 + c) * 32
    grad_second = ((1 - z % 2) * 4 + x) * 256 + (y * 2 + c) * 32

    def relative(column):
        place = column // width
        return (((place // 8) ^ yl) * 8 + ((place // 2 % 4) ^ x) * 2 + ((place % 2) ^ c)) * width + column % width

    first = relative(jnp.where(is_act, act_first, grad_first))
    second = relative(jnp.where(is_act, act_first + 32, grad_second))
    pair = jnp.where(z % 2 == 1, z + 1, z - 1) % 8
    done = whitened_columns(
        pieces,
        jnp.stack([first, second, yh, c, jnp.where(c == 0, z, pair), jnp.where(c == 0, pair, z)]),
        block,
        token_count,
    )

    done, over_x = lax.optimization_barrier((done, over_x))
    input_grad = grads_by_weight(jnp.stack([yl, x, c]).astype(jnp.int32), over_x, weight)

    swapped = xor_swap(done, "z", 1)
    grads = jnp.where(is_act, swapped[32:], done[:32])
    acts = jnp.where(is_act, done, swapped)
    grads = {0: grads, **{m: y_swap(grads, m) for m in (1, 3, 2)}}
    acts = {0: acts, **{m: xor_swap(acts, "x", m) for m in (1, 3, 2)}}
    grads = jnp.concatenate([grads[m] for m in range(4)])
    acts = jnp.concatenate([acts[m] for m in range(4)])
    grads, acts, input_grad = lax.optimization_barrier((grads, acts, input_grad))
    numbers = jnp.stack([y * 2 + c, x]).astype(jnp.int32)
    tile = update_tile(numbers, acts, grads, xor_swap(grads, "c", 1))
    tile = lax.ppermute(tile, ("z", "yl", "c"), owners())
    own, give = jnp.where(c == 0, tile[0], tile[1]), jnp.where(c == 0, tile[1], tile[0])
    other = xor_swap(give, "c", 1)
    update = jnp.stack([jnp.where(c == 0, own, other), jnp.where(c == 0, other, own)], axis=1)
    return update, input_grad.transpose(1, 0, 2)


def solution(mesh):
    split = Mesh(
        mesh.devices.reshape(mesh.shape["tok"], 2, 4, 2, mesh.shape["grp"]),
        ("z", "yl", "x", "c", "yh"),
    )
    out = ("yl", "x", "c")
    in_specs = (P(("z", "yh"), None, out), P(("z", "yh"), None, out), P(None, out, None))
    out_specs = (P(("z", "yh"), None, out), P(("z", "yh"), None, out))
    return jax.shard_map(local, mesh=split, in_specs=in_specs, out_specs=out_specs, check_vma=False)
```

```python
import math

import jax
import jax.numpy as jnp
from jax import lax
from jax.experimental import pallas as pl
from jax.experimental.pallas import tpu as pltpu
from jax.sharding import Mesh
from jax.sharding import PartitionSpec as P

DAMPING = 0.1
COLUMNS = 64
F32 = jnp.float32
BF16 = jnp.bfloat16


def split2(value):
    high = value.astype(BF16)
    low = (value - high.astype(F32)).astype(BF16)
    return high, low


def split3(value):
    high = value.astype(BF16)
    rest = value - high.astype(F32)
    middle = rest.astype(BF16)
    low = (rest - middle.astype(F32)).astype(BF16)
    return high, middle, low


def chain_kernel(where, *refs):
    pieces = refs[:10]
    out, side, turned, now, later, f1, f2, f3, u1, u2, sems = refs[10:]
    block, tokens = turned.shape
    half = COLUMNS // 2
    copies = []
    for source, row, col in placed(pieces, where[3] == 0):
        row, col = pl.multiple_of(row, 512), pl.multiple_of(col, 128)
        to = side.at[pl.ds(row, 512), pl.ds(col, 128)]
        copies.append((pltpu.make_async_copy(source, to, sems.at[len(copies)]), row, col))
        copies[-1][0].start()
    now[...] = jnp.zeros_like(now)
    later[...] = jnp.zeros_like(later)
    for copy, row, col in copies:
        copy.wait()
        turned[pl.ds(col, 128), pl.ds(row, 512)] = side[pl.ds(row, 512), pl.ds(col, 128)].T

    probe_at = pl.ds(2 * COLUMNS, 16)
    probe_row = lax.broadcasted_iota(jnp.int32, (16, block), 0)

    def times(rows, matrix):
        product = jnp.dot(rows[...], matrix[...], preferred_element_type=F32)
        probe = jnp.sum(product[2 * COLUMNS :], axis=0, keepdims=True)
        return product[:COLUMNS] + product[COLUMNS : 2 * COLUMNS], probe

    def keep(target, rows, probe=None):
        target[:COLUMNS], target[COLUMNS : 2 * COLUMNS] = split2(rows)
        if probe is not None:
            high, middle, low = (part.astype(F32) for part in split3(probe))
            stacked = jnp.where(probe_row == 0, high, jnp.where(probe_row == 1, middle, low))
            target[probe_at] = jnp.where(probe_row < 3, stacked, 0.0).astype(BF16)

    def unit():
        row = lax.broadcasted_iota(jnp.int32, (COLUMNS, block), 0)
        wanted = jnp.where(row < half, where[0] + row, where[1] + row - half)
        col = lax.broadcasted_iota(jnp.int32, (COLUMNS, block), 1)
        return jnp.where(col == wanted, 1.0, 0.0)

    later[:half] = turned[pl.ds(pl.multiple_of(where[0], half), half), :]
    later[half:COLUMNS] = turned[pl.ds(pl.multiple_of(where[1], half), half), :]
    rows, _ = times(later, side)
    rows = rows / tokens + DAMPING * unit()
    f1[...] = rows
    keep(now, rows, jnp.ones((1, block), F32))
    keep(later, *times(now, turned))
    rows, probe = times(later, side)
    rows, probe = rows / tokens + DAMPING * f1[...], probe / tokens + DAMPING
    f2[...], u1[...] = rows, probe
    keep(now, rows, probe)
    keep(later, *times(now, turned))
    rows, probe = times(later, side)
    rows, probe = rows / tokens + DAMPING * f2[...], probe / tokens + DAMPING * u1[...]
    f3[...], u2[...] = rows, probe
    keep(now, rows, probe)
    rows, probe = times(now, turned)
    keep(later, rows)
    norm = jnp.sum(u2[...] * u2[...], axis=1, keepdims=True)
    scale = (jnp.sum(probe * probe, axis=1, keepdims=True) / tokens + DAMPING * norm) / norm
    inverse = 1.0 / scale
    inverse2 = inverse * inverse
    rows, _ = times(later, side)
    a3 = f3[...] * (inverse2 * inverse)
    a4 = (rows / tokens) * (inverse2 * inverse2) + DAMPING * (a3 * inverse)
    total = 36.0 * unit() - 39.0 * (f1[...] * inverse) + 27.0 * (f2[...] * inverse2)
    keep(now, (total - 9.0 * a3 + a4) * (1.0 / (16.0 * jnp.sqrt(scale))))
    rows, _ = times(now, turned)
    for at in range(16):
        z = (where[4 + at // 4 % 2] - 2 * (at % 4)) % 8
        to = pl.ds(pl.multiple_of(((at // 8) ^ where[2]) * 1024 + z * 128, 128), 128)
        out[:, to] = rows[:, at * 128 : at * 128 + 128].astype(BF16)


def placed(pieces, first_core):
    for core in range(2):
        for outer in range(4):
            for inner in range(4):
                for other in range(2):
                    piece = core * 5 + outer + (outer == 3 or outer == 2 and inner >= 2)
                    part = pieces[piece].at[pl.ds(((inner % 2 if outer == 2 else inner) * 2 + other) * 512, 512)]

                    def spot(x, y):
                        return y // 2 * 1024 + core * 512, (y % 2 * 8 + x * 2) * 128

                    x_first, y_first = spot(inner, outer), spot(outer, inner)
                    if core:
                        x_first, y_first = y_first, x_first
                    row, col = (jnp.where(first_core, p, q) for p, q in zip(x_first, y_first))
                    yield part, row, col + (core ^ other) * 128


def whitened_columns(pieces, where, block, tokens):
    rows = 2 * COLUMNS + 16
    passes = 8 * 2 * rows * block * tokens
    return pl.pallas_call(
        chain_kernel,
        name="whiten",
        out_shape=jax.ShapeDtypeStruct((COLUMNS, tokens), BF16),
        in_specs=[pl.BlockSpec(memory_space=pltpu.SMEM)] + [pl.BlockSpec(memory_space=pl.ANY)] * 10,
        out_specs=pl.BlockSpec(memory_space=pltpu.VMEM),
        scratch_shapes=[
            pltpu.VMEM((tokens, block), BF16),
            pltpu.VMEM((block, tokens), BF16),
            pltpu.VMEM((rows, block), BF16),
            pltpu.VMEM((rows, tokens), BF16),
            *[pltpu.VMEM((COLUMNS, block), F32)] * 3,
            *[pltpu.VMEM((1, block), F32)] * 2,
            pltpu.SemaphoreType.DMA((64,)),
        ],
        compiler_params=pltpu.CompilerParams(vmem_limit_bytes=32 * 2**20),
        cost_estimate=pl.CostEstimate(flops=passes, bytes_accessed=2 * block * tokens, transcendentals=0),
    )(where, *pieces)


def xor_swap(array, axis, mask):
    return lax.ppermute(array, axis, [(i, i ^ mask) for i in range(lax.axis_size(axis))])


def y_swap(array, mask):
    pairs = [(y % 2 * 2 + y // 2, (y ^ mask) % 2 * 2 + (y ^ mask) // 2) for y in range(4)]
    return lax.ppermute(array, ("yl", "yh"), pairs)


def plane_swap(array, first_mask, second_mask):
    def at(x, y, c):
        return (((y % 2) * 4 + x) * 2 + c) * 2 + y // 2

    pairs = []
    for x in range(4):
        for y in range(4):
            pairs.append((at(x, y, 0), at(x ^ first_mask, y ^ second_mask, 0)))
            pairs.append((at(x, y, 1), at(x ^ second_mask, y ^ first_mask, 1)))
    return lax.ppermute(array, ("yl", "x", "c", "yh"), pairs)


def twin(z):
    return (z + 1 if z % 2 else z - 1) % 8


def shared_part(activations, out_grads, z, c):
    turn = (z + 1) // 2 % 4
    pieces = (activations[:, 0], out_grads[:, 0], activations[:, 1], out_grads[:, 1])
    odd, far = turn % 2 == 1, turn >= 2
    pieces = [jnp.where(odd, pieces[(j + 1) % 4], pieces[j]) for j in range(4)]
    pieces = [jnp.where(far, pieces[(j + 2) % 4], pieces[j]) for j in range(4)]
    got = [pieces[0]]
    for shift in (1, 2, 3):
        got.append(lax.ppermute(pieces[shift], "z", [(i, (i + 2 * shift) % 8) for i in range(8)]))
    got = jnp.concatenate(got)
    across, beside = [], []
    for i in range(8):
        across += [(i * 2, twin(i) * 2 + 1), (i * 2 + 1, i * 2)]
        beside.append((i * 2 + 1, twin(i) * 2 + 1))
    one = lax.ppermute(got, ("z", "c"), across)
    two = lax.ppermute(got, ("z", "c"), beside)
    return jnp.concatenate([jnp.where(c == 0, got, two), one])


def side_pieces(part):
    masks = (1, 3, 2)
    step = {0: part, **{m: plane_swap(part, m, 0) for m in masks}}
    row = jnp.concatenate([step[m] for m in range(4)])
    one, three = plane_swap(row, 0, 1), plane_swap(row, 0, 3)
    two = [plane_swap(one[:2048], 0, 3), plane_swap(three[2048:], 0, 1)]
    return [row, one, *two, three]


def tile_kernel(where, acts, own, other, out, grads):
    tokens = grads.shape[1]
    for core, part in enumerate((own, other)):
        for at in range(4):
            row = pl.multiple_of(((at * 2 + core) ^ where[0]) * 32, 32)
            grads[pl.ds(row, 32), :] = part[at * 32 : at * 32 + 32, :]
    product = lax.dot_general(acts[...], grads[...], (((1,), (1,)), ((), ())), preferred_element_type=F32)
    product = (product / math.sqrt(tokens)).astype(BF16)
    for at in range(4):
        row = pl.multiple_of((at ^ where[1]) * 64, 64)
        for core in range(2):
            out[core, pl.ds(row, 64), :] = product[at * 64 : at * 64 + 64, core * 128 : core * 128 + 128]


def update_tile(where, acts, own, other):
    tokens = own.shape[1]
    return pl.pallas_call(
        tile_kernel,
        name="update_tile",
        out_shape=jax.ShapeDtypeStruct((2, 256, 128), BF16),
        in_specs=[pl.BlockSpec(memory_space=pltpu.SMEM)] + [pl.BlockSpec(memory_space=pltpu.VMEM)] * 3,
        out_specs=pl.BlockSpec(memory_space=pltpu.VMEM),
        scratch_shapes=[pltpu.VMEM((256, tokens), BF16)],
        compiler_params=pltpu.CompilerParams(vmem_limit_bytes=16 * 2**20),
        cost_estimate=pl.CostEstimate(flops=2 * 256 * 256 * tokens, bytes_accessed=2**21, transcendentals=0),
    )(where, acts, own, other)


def input_kernel(where, *refs):
    parts, weight, out, grads = refs[:4], refs[4], refs[5], refs[6]
    for x in range(4):
        for yl in range(2):
            for core in range(2):
                spot = (yl ^ where[0]) * 1024 + (x ^ where[1]) * 256 + (core ^ where[2]) * 128
                for side in range(2):
                    row = ((yl * 2 + core) * 2 + side) * 128
                    col = pl.multiple_of(side * 2048 + spot, 128)
                    grads[:, pl.ds(col, 128)] = parts[x][row : row + 128, :]
    product = lax.dot_general(grads[...], weight[...], (((1,), (1,)), ((), ())), preferred_element_type=F32)
    for side in range(2):
        out[side] = product[:, side * 128 : side * 128 + 128].astype(BF16)


def grads_by_weight(where, parts, weight):
    blocks, width, features = weight.shape
    tokens = parts[0].shape[0] // 8
    return pl.pallas_call(
        input_kernel,
        name="input_grad",
        out_shape=jax.ShapeDtypeStruct((blocks, tokens, width), BF16),
        in_specs=[pl.BlockSpec(memory_space=pltpu.SMEM)] + [pl.BlockSpec(memory_space=pltpu.VMEM)] * 5,
        out_specs=pl.BlockSpec(memory_space=pltpu.VMEM),
        scratch_shapes=[pltpu.VMEM((tokens, features), BF16)],
        compiler_params=pltpu.CompilerParams(vmem_limit_bytes=16 * 2**20),
        cost_estimate=pl.CostEstimate(
            flops=2 * tokens * features * blocks * width, bytes_accessed=3 * 2**20, transcendentals=0
        ),
    )(where, *parts, weight.reshape(blocks * width, features))


def owners():
    pairs = []
    for z in range(8):
        act_side, grad_side = (0, 1, 1, 0)[z // 2], z // 4
        for yl in range(2):
            for c in range(2):
                to = ((act_side * 4 + yl * 2 + c) * 2 + z % 2) * 2 + grad_side
                pairs.append(((z * 2 + yl) * 2 + c, to))
    return pairs


def local(activations, out_grads, weight):
    tok_dev, blocks, width = activations.shape
    outs = lax.axis_size(("yl", "x", "c"))
    block = width * outs
    z, yl, x, c, yh = (lax.axis_index(a) for a in ("z", "yl", "x", "c", "yh"))
    token_count = tok_dev * lax.axis_size("z") * lax.axis_size("yh")

    pieces = side_pieces(shared_part(activations, out_grads, z, c))
    pieces += [xor_swap(piece, "c", 1) for piece in pieces]
    near = jnp.concatenate([out_grads[:, 0], out_grads[:, 1]])
    near = jnp.concatenate([near, xor_swap(near, "c", 1)])
    near = jnp.concatenate([near, xor_swap(near, "yl", 1)])
    near, pieces = lax.optimization_barrier((near, pieces))
    over_x = [near] + [xor_swap(near, "x", m) for m in (1, 2, 3)]

    y = yh * 2 + yl
    is_act = (z + 1) // 2 % 2 == 0
    act_first = ((yl * 2 + c) * 2 + yh) * 256 + x * 64
    grad_first = (z % 2 * 4 + x) * 256 + (y * 2 + c) * 32
    grad_second = ((1 - z % 2) * 4 + x) * 256 + (y * 2 + c) * 32

    def relative(column):
        place = column // width
        return (((place // 8) ^ yl) * 8 + ((place // 2 % 4) ^ x) * 2 + ((place % 2) ^ c)) * width + column % width

    first = relative(jnp.where(is_act, act_first, grad_first))
    second = relative(jnp.where(is_act, act_first + 32, grad_second))
    pair = jnp.where(z % 2 == 1, z + 1, z - 1) % 8
    done = whitened_columns(
        pieces,
        jnp.stack([first, second, yh, c, jnp.where(c == 0, z, pair), jnp.where(c == 0, pair, z)]),
        block,
        token_count,
    )

    done, over_x = lax.optimization_barrier((done, over_x))
    input_grad = grads_by_weight(jnp.stack([yl, x, c]).astype(jnp.int32), over_x, weight)

    swapped = xor_swap(done, "z", 1)
    acts = jnp.where(is_act, done, swapped)
    grads = jnp.where(is_act, swapped[32:], done[:32])
    acts = {0: acts, **{m: xor_swap(acts, "x", m) for m in (1, 3, 2)}}
    grads = {0: grads, 1: y_swap(grads, 1)}
    pair = y_swap(jnp.concatenate([grads[0], grads[1]]), 2)
    grads |= {2: pair[:32], 3: pair[32:]}
    grads = jnp.concatenate([grads[m] for m in range(4)])
    acts = jnp.concatenate([acts[m] for m in range(4)])
    grads, acts, input_grad = lax.optimization_barrier((grads, acts, input_grad))
    numbers = jnp.stack([y * 2 + c, x]).astype(jnp.int32)
    tile = update_tile(numbers, acts, grads, xor_swap(grads, "c", 1))
    tile = lax.ppermute(tile, ("z", "yl", "c"), owners())
    own, give = jnp.where(c == 0, tile[0], tile[1]), jnp.where(c == 0, tile[1], tile[0])
    other = xor_swap(give, "c", 1)
    update = jnp.stack([jnp.where(c == 0, own, other), jnp.where(c == 0, other, own)], axis=1)
    return update, input_grad.transpose(1, 0, 2)


def solution(mesh):
    split = Mesh(
        mesh.devices.reshape(mesh.shape["tok"], 2, 4, 2, mesh.shape["grp"]),
        ("z", "yl", "x", "c", "yh"),
    )
    out = ("yl", "x", "c")
    in_specs = (P(("z", "yh"), None, out), P(("z", "yh"), None, out), P(None, out, None))
    out_specs = (P(("z", "yh"), None, out), P(("z", "yh"), None, out))
    return jax.shard_map(local, mesh=split, in_specs=in_specs, out_specs=out_specs, check_vma=False)
```
